32 devices in a mesh: ctx: 8 (over y, x, core), exp: 4 (over z).
Axes of the slice: x: 2, y: 2, z: 4, core: 2. Of those that a mesh axis runs over, the one named last changes fastest.
Arguments:
- tokens: bfloat16 [4096, 2048], P(('ctx', 'exp')), may hold values from -6 to 6
- cotangent: bfloat16 [4096, 2048], P(('ctx', 'exp')), may hold values from -6 to 6
- expert_ids: int32 [4096, 1], P(('ctx', 'exp')), may hold values from 0 to 3; in each aligned block of 128 rows (0 to 127, 128 to 255, ...) at most 48 rows name the same one
- route_weights: float32 [4096, 1], P(('ctx', 'exp')), may hold values from 0.1 to 1
- w_gate: bfloat16 [4, 2048, 768], P('exp', 'ctx'), may hold values from -0.125 to 0.125
- w_up: bfloat16 [4, 2048, 768], P('exp', 'ctx'), may hold values from -0.125 to 0.125
- w_down: bfloat16 [4, 768, 2048], P('exp', None, 'ctx'), may hold values from -0.21875 to 0.21875
Outputs:
- token_grads: bfloat16 [4096, 2048], P(('ctx', 'exp'))
- route_grads: float32 [4096, 1], P(('ctx', 'exp'))
- gate_grads: bfloat16 [4, 2048, 768], P('exp', 'ctx')
- up_grads: bfloat16 [4, 2048, 768], P('exp', 'ctx')
- down_grads: bfloat16 [4, 768, 2048], P('exp', None, 'ctx')
The draws below stay inside these ranges and needn't reach their ends.
Inputs may be any that keep to these rules, and one draw needn't show every extreme that they name: `expert_ids`: among the 128 routes of one device's tokens no expert is named more than 48 times, a bound that some block reaches; the routes of one token name different experts.
All inputs are finite; a program needn't handle non-finite values.
Results may differ from the reference program's by a relative error of at most 0.018.
Values may be sent and summed in bfloat16 or wider, within the bound.
A program may use at most 64 MiB of HBM per device.

```python
import math
import jax
import jax.numpy as jnp
import numpy as np
from jax import lax

D = 2048
FF = 768
TOK_DEV = 128
ROUTES = 1
EXPERTS = 4
CAP = 48
TOKENS = 4096
N_CTX = 8
N_EXP = 4


def levels(own_key, shape, split, low, high):
    def one(axis_at, blocks):
        heights = jax.random.uniform(jax.random.fold_in(jax.random.fold_in(own_key, 6), axis_at), (blocks,), jnp.float32, low / len(split), high / len(split))
        return jnp.repeat(jnp.exp(heights), shape[axis_at] // blocks).reshape((-1,) + (1,) * (len(shape) - axis_at - 1))

    loudness = one(*split[0])
    for cut in split[1:]:
        loudness = loudness * one(*cut)
    return loudness


def routed_block(own_key, own, number, rows, number_of, top, reach, slope):
    sequence = jax.random.permutation(own_key, number_of)
    crowded, ordinary = portions_of(number_of, rows * top, reach, slope, True), portions_of(number_of, rows * top, reach, slope, False)
    places = jnp.arange(number_of)

    def named(sizes, turn):
        used = int((sizes > 0).sum())
        fixed = max(1, used // 4)
        moved = fixed + (places - fixed + turn * (used - fixed)) % max(1, number_of - fixed)
        return jnp.zeros((number_of,), jnp.int32).at[sequence[jnp.where(places < fixed, places, moved)]].set(jnp.asarray(sizes, jnp.int32))

    sizes = jnp.where(number % 4 == 0, named(crowded, number // 4), named(ordinary, number - number // 4 - 1))
    mixed = jax.random.permutation(jax.random.fold_in(own, 3), number_of)
    donor, receiver = mixed[0:number_of // 2 * 2:2], mixed[1:number_of // 2 * 2:2]
    slack = jnp.minimum(sizes[donor] - 1, reach - sizes[receiver]) // 2
    slack = jnp.where((donor == sequence[0]) | (receiver == sequence[0]) | (sizes[receiver] == 0), 0, jnp.maximum(slack, 0))
    moved = jax.random.randint(jax.random.fold_in(own, 4), (number_of // 2,), 0, 1 << 20) % (slack + 1)
    sizes = sizes.at[donor].add(-moved).at[receiver].add(moved)
    items = jnp.searchsorted(jnp.cumsum(sizes), jnp.arange(rows * top), side="right").astype(jnp.int32)
    grid = items.reshape(top, rows).T
    grid = grid[jax.random.permutation(jax.random.fold_in(own, 1), rows)]
    turn = jax.random.randint(jax.random.fold_in(own, 2), (rows, 1), 0, top)
    return jnp.take_along_axis(grid, (jnp.arange(top)[None, :] + turn) % top, axis=1)


def portions_of(count, total, bound, slope, full):
    portions = [(1 << 20) // math.isqrt(rank ** slope) + 1 for rank in range(1, count + 1)]
    largest = bound if full else min(bound, max(-(-total // count), total * portions[0] // sum(portions)))
    least = 1 if total - largest >= count - 1 else 0
    given, rest = [largest] + [least] * (count - 1), total - largest - least * (count - 1)
    while rest > 0:
        movable = [i for i in range(1, count) if given[i] < largest] or [i for i in range(1, count) if given[i] < bound]
        whole, budget = sum([portions[i] for i in movable]), rest
        for i in movable:
            addition = min(bound - given[i], max(1, budget * portions[i] // whole), rest)
            given[i] = given[i] + addition
            rest = rest - addition
    return np.array(given)


def gaussian(rng, extent, deviation, limit, shards=(), held_as=jnp.bfloat16):
    drawn = jax.random.normal(rng, extent, jnp.float32) * deviation
    if len(shards) > 0:
        drawn = levels(rng, extent, shards, -0.22, 0.18) * drawn
    return jnp.clip(drawn, min=-limit, max=limit).astype(held_as)


def setup_inputs(seed: int = 0) -> dict:
    streams_of = jax.random.split(jax.random.key(seed), 8)
    tokens = gaussian(streams_of[0], (TOKENS, D), 1.0, 6.0, ((0, 32),))
    cotangent = gaussian(streams_of[1], (TOKENS, D), 1.0, 6.0, ((0, 32),))
    expert_ids_keys = jax.random.split(jax.random.fold_in(streams_of[2], 1), TOKENS // TOK_DEV)
    expert_ids_turns = jax.random.permutation(jax.random.fold_in(streams_of[2], 3), TOKENS // TOK_DEV)
    expert_ids = jax.vmap(lambda own, number: routed_block(jax.random.fold_in(streams_of[2], 2), own, number, TOK_DEV, EXPERTS, ROUTES, CAP, 2))(expert_ids_keys, expert_ids_turns).reshape((TOKENS, ROUTES))
    route_weights = jnp.clip(jnp.exp(math.log(1.0) - 2.3025851 * jax.random.uniform(streams_of[3], (TOKENS, ROUTES), jnp.float32) ** levels(streams_of[3], (TOKENS, ROUTES), ((0, 32),), -0.2, 0.2)), 0.1, 1.0)
    w_gate = gaussian(streams_of[4], (EXPERTS, D, FF), D ** -0.5, 0.125, ((0, 4), (1, 8)))
    w_up = gaussian(streams_of[5], (EXPERTS, D, FF), D ** -0.5, 0.125, ((0, 4), (1, 8)))
    w_down = gaussian(streams_of[6], (EXPERTS, FF, D), FF ** -0.5, 0.21875, ((0, 4), (2, 8)))
    return dict(tokens=tokens, cotangent=cotangent, expert_ids=expert_ids, route_weights=route_weights, w_gate=w_gate, w_up=w_up, w_down=w_down)


def reference(tokens, cotangent, expert_ids, route_weights, w_gate, w_up, w_down):
    device_count = N_CTX * N_EXP
    slot_count = TOK_DEV * ROUTES
    per_expert = device_count * CAP
    col_count = D // N_CTX
    route_ids = expert_ids.reshape(device_count, slot_count)
    labels = jnp.arange(EXPERTS, dtype=jnp.int32)
    onehot = (route_ids[:, :, None] == labels[None, None, :]).astype(jnp.int32)
    position = jnp.sum((jnp.cumsum(onehot, axis=1) - 1) * onehot, axis=2)
    source = jnp.arange(device_count, dtype=jnp.int32)[:, None]
    target = (route_ids * per_expert + source * CAP + position).reshape(-1).astype(jnp.int32)
    token_slots = jnp.repeat(tokens, ROUTES, axis=0)
    scaled = (route_weights.reshape(-1, 1) * jnp.repeat(cotangent, ROUTES, axis=0).astype(jnp.float32)).astype(jnp.bfloat16)
    x_buffer = jnp.zeros((EXPERTS * per_expert, D), jnp.bfloat16).at[target].set(token_slots).reshape(EXPERTS, per_expert, D)
    y_buffer = jnp.zeros((EXPERTS * per_expert, D), jnp.bfloat16).at[target].set(scaled).reshape(EXPERTS, per_expert, D)

    def one_expert(bundle):
        slot_x, slot_y, gate_weight, up_weight, down_weight = bundle
        x_blocks = slot_x.reshape(per_expert, N_CTX, col_count).astype(jnp.float32)
        y_blocks = slot_y.reshape(per_expert, N_CTX, col_count).astype(jnp.float32)
        both = jnp.concatenate([gate_weight, up_weight], axis=1).reshape(N_CTX, col_count, 2 * FF).astype(jnp.float32)
        parts = jnp.einsum("rcd,cdf->crf", x_blocks, both).astype(jnp.bfloat16)
        totals = jnp.sum(parts.astype(jnp.float32), axis=0)
        gate_pre = totals[:, :FF]
        up_pre = totals[:, FF:]
        gate_sig = jax.nn.sigmoid(gate_pre)
        hidden = (gate_pre * gate_sig * up_pre).astype(jnp.bfloat16)
        outputs = jnp.dot(hidden, down_weight, preferred_element_type=jnp.float32)
        inner_part = jnp.sum(slot_y.astype(jnp.float32) * outputs, axis=1)
        down_blocks = down_weight.reshape(FF, N_CTX, col_count).astype(jnp.float32)
        back_parts = jnp.einsum("rcd,fcd->crf", y_blocks, down_blocks).astype(jnp.bfloat16)
        back_sum = jnp.sum(back_parts.astype(jnp.float32), axis=0)
        d_up = (back_sum * gate_pre * gate_sig).astype(jnp.bfloat16)
        d_gate = (back_sum * up_pre * gate_sig * (1.0 + gate_pre * (1.0 - gate_sig))).astype(jnp.bfloat16)
        down_grad = jnp.dot(hidden.T, slot_y, preferred_element_type=jnp.float32).astype(jnp.bfloat16)
        gate_grad = jnp.dot(slot_x.T, d_gate, preferred_element_type=jnp.float32).astype(jnp.bfloat16)
        up_grad = jnp.dot(slot_x.T, d_up, preferred_element_type=jnp.float32).astype(jnp.bfloat16)
        slot_grad = (jnp.dot(d_gate, gate_weight.T, preferred_element_type=jnp.float32)
                     + jnp.dot(d_up, up_weight.T, preferred_element_type=jnp.float32)).astype(jnp.bfloat16)
        return gate_grad, up_grad, down_grad, slot_grad, inner_part

    gate_grads, up_grads, down_grads, slot_grads, inner_all = lax.map(
        one_expert, (x_buffer, y_buffer, w_gate, w_up, w_down))
    picked = slot_grads.reshape(EXPERTS * per_expert, D)[target]
    token_grads = jnp.sum(picked.reshape(TOKENS, ROUTES, D).astype(jnp.float32), axis=1).astype(jnp.bfloat16)
    route_grads = inner_all.reshape(-1)[target].reshape(TOKENS, ROUTES) / route_weights
    return token_grads, route_grads, gate_grads, up_grads, down_grads
```

```python
import functools

import jax
import jax.numpy as jnp
from jax import lax
from jax.experimental import pallas as pl
from jax.experimental.pallas import tpu as pltpu
from jax.sharding import PartitionSpec as P

MESH = pl.DeviceIdType.MESH


def slot_table(route_ids, expert_count, capacity):
    labels = jnp.arange(expert_count, dtype=jnp.int32)
    onehot = (route_ids[..., :, None] == labels).astype(jnp.int32)
    position = jnp.sum((jnp.cumsum(onehot, axis=-2) - 1) * onehot, axis=-1)
    target = route_ids * capacity + position
    places = jnp.arange(expert_count * capacity, dtype=jnp.int32)
    return (target[..., None, :] == places[:, None]).astype(jnp.bfloat16)


def forward_hidden(totals, units):
    gate_pre = totals[:, :units]
    up_pre = totals[:, units:]
    gate_sig = jax.nn.sigmoid(gate_pre)
    return (gate_pre * gate_sig * up_pre).astype(jnp.bfloat16)


def backward_grads(totals, back_sum, units):
    gate_pre = totals[:, :units]
    up_pre = totals[:, units:]
    gate_sig = jax.nn.sigmoid(gate_pre)
    d_up = (back_sum * gate_pre * gate_sig).astype(jnp.bfloat16)
    d_gate = (back_sum * up_pre * gate_sig * (1.0 + gate_pre * (1.0 - gate_sig))).astype(
        jnp.bfloat16
    )
    return jnp.concatenate([d_gate, d_up], axis=1)


def body(tokens, cotangent, expert_ids, route_weights, w_gate, w_up, w_down):
    ctx_size = lax.axis_size("ctx")
    exp_size = lax.axis_size("exp")
    tok_count, model_width = tokens.shape
    route_count = expert_ids.shape[1]
    slot_count = tok_count * route_count
    expert_count = w_gate.shape[0] * exp_size
    capacity = max(2, (3 * slot_count + 2 * expert_count - 1) // (2 * expert_count))
    col_count = model_width // ctx_size
    units = w_gate.shape[2]
    row_count = ctx_size * exp_size * capacity
    own_rows = row_count // ctx_size
    all_ids = lax.all_gather(expert_ids, "ctx", axis=0, tiled=True)
    tables = slot_table(all_ids.reshape(ctx_size, slot_count), expert_count, capacity)
    token_slots = jnp.repeat(tokens, route_count, axis=0)
    scaled = (
        route_weights * jnp.repeat(cotangent, route_count, axis=0).astype(jnp.float32)
    ).astype(jnp.bfloat16)
    own_table = lax.dynamic_index_in_dim(tables, lax.axis_index("ctx"), 0, keepdims=False)
    send_x = jnp.dot(own_table, token_slots, preferred_element_type=jnp.float32).astype(
        jnp.bfloat16
    )
    send_y = jnp.dot(own_table, scaled, preferred_element_type=jnp.float32).astype(jnp.bfloat16)
    send_x = send_x.reshape(expert_count, capacity, model_width)
    send_y = send_y.reshape(expert_count, capacity, model_width)
    group_x, group_y = (
        lax.all_to_all(send_x, "exp", split_axis=0, concat_axis=0, tiled=True),
        lax.all_to_all(send_y, "exp", split_axis=0, concat_axis=0, tiled=True),
    )
    slot_x, slot_y = (
        lax.all_to_all(group_x, "ctx", split_axis=2, concat_axis=0, tiled=True),
        lax.all_to_all(group_y, "ctx", split_axis=2, concat_axis=0, tiled=True),
    )
    slot_x = slot_x.reshape(row_count, col_count)
    slot_y = slot_y.reshape(row_count, col_count)
    gate_weight = w_gate[0]
    up_weight = w_up[0]
    down_weight = w_down[0]
    both_weights = jnp.concatenate([gate_weight, up_weight], axis=1)

    def fold_grad(segment):
        gate_acc = lax.dot_general(
            slot_x, segment[:, :units], (((0,), (0,)), ((), ())), preferred_element_type=jnp.float32
        )
        up_acc = lax.dot_general(
            slot_x, segment[:, units:], (((0,), (0,)), ((), ())), preferred_element_type=jnp.float32
        )
        grad_rows = lax.dot_general(
            segment, both_weights, (((1,), (1,)), ((), ())), preferred_element_type=jnp.float32
        )
        return (gate_acc, up_acc, grad_rows)

    row_x, row_y = (
        lax.all_to_all(slot_x, "ctx", split_axis=0, concat_axis=1, tiled=True),
        lax.all_to_all(slot_y, "ctx", split_axis=0, concat_axis=1, tiled=True),
    )
    full_gate, full_up, full_down = (
        lax.all_gather(gate_weight, "ctx", axis=0, tiled=True),
        lax.all_gather(up_weight, "ctx", axis=0, tiled=True),
        lax.all_gather(down_weight, "ctx", axis=1, tiled=True),
    )
    full_both = jnp.concatenate([full_gate, full_up], axis=1).reshape(
        ctx_size, col_count, 2 * units
    )
    gate_blocks = jnp.einsum(
        "rcd,cdf->crf",
        row_x.reshape(own_rows, ctx_size, col_count),
        full_both,
        preferred_element_type=jnp.float32,
    ).astype(jnp.bfloat16)
    totals_own = jnp.sum(gate_blocks.astype(jnp.float32), axis=0)
    hidden_own = forward_hidden(totals_own, units)
    back_blocks = jnp.einsum(
        "rcd,fcd->crf",
        row_y.reshape(own_rows, ctx_size, col_count),
        full_down.reshape(units, ctx_size, col_count),
        preferred_element_type=jnp.float32,
    ).astype(jnp.bfloat16)
    back_own = jnp.sum(back_blocks.astype(jnp.float32), axis=0)
    grads_own = backward_grads(totals_own, back_own, units)
    segment = (
        lax.all_gather(hidden_own, "ctx", axis=0, tiled=True),
        lax.all_gather(grads_own, "ctx", axis=0, tiled=True),
    )
    fold_segment = segment[0]
    outputs = jnp.dot(fold_segment, down_weight, preferred_element_type=jnp.float32)
    inner_rows = jnp.sum(slot_y.astype(jnp.float32) * outputs, axis=1)
    inner_all = inner_rows
    down_acc = lax.dot_general(
        fold_segment, slot_y, (((0,), (0,)), ((), ())), preferred_element_type=jnp.float32
    )
    down_state = (down_acc, inner_all)
    grad_state = fold_grad(segment[1])
    down_acc = down_state[0]
    inner_all = down_state[1]
    gate_acc = grad_state[0]
    up_acc = grad_state[1]
    back_rows = grad_state[2]
    back_slots = back_rows.astype(jnp.bfloat16).reshape(ctx_size, exp_size, capacity, col_count)
    inner_slots = inner_all.reshape(ctx_size, exp_size, capacity)
    home_back = lax.all_to_all(back_slots, "exp", split_axis=1, concat_axis=1, tiled=True)
    home_inner = lax.all_to_all(inner_slots, "exp", split_axis=1, concat_axis=1, tiled=True)
    merged = jnp.einsum(
        "cks,ckd->csd",
        tables,
        home_back.reshape(ctx_size, expert_count * capacity, col_count),
        preferred_element_type=jnp.float32,
    )
    merged = jnp.sum(merged.reshape(ctx_size, tok_count, route_count, col_count), axis=2).astype(
        jnp.bfloat16
    )
    grads_home = lax.all_to_all(merged, "ctx", split_axis=0, concat_axis=2, tiled=True)
    token_grads = grads_home.reshape(tok_count, model_width)
    inner_home = jnp.einsum(
        "cks,ck->cs",
        tables.astype(jnp.float32),
        home_inner.reshape(ctx_size, expert_count * capacity),
        precision=lax.Precision.HIGHEST,
    )
    route_sums = lax.psum_scatter(inner_home, "ctx", scatter_dimension=0, tiled=True).reshape(
        tok_count, route_count
    )
    route_grads = route_sums / route_weights
    gate_grads = gate_acc.astype(jnp.bfloat16)[None]
    up_grads = up_acc.astype(jnp.bfloat16)[None]
    down_grads = down_acc.astype(jnp.bfloat16)[None]
    return (token_grads, route_grads, gate_grads, up_grads, down_grads)


def ctx_neighbours(me):
    sib = me + 1 - 2 * (me % 2)
    across = me + 2 - 4 * ((me // 2) % 2)
    along = me + 4 - 8 * ((me // 4) % 2)
    return sib, across, along


def enter(ctx_peers, exp_peers):
    barrier = pltpu.get_barrier_semaphore()
    for peer in ctx_peers:
        pl.semaphore_signal(barrier, inc=1, device_id={"ctx": peer}, device_id_type=MESH)
    for peer in exp_peers:
        pl.semaphore_signal(barrier, inc=1, device_id={"exp": peer}, device_id_type=MESH)
    pl.semaphore_wait(barrier, len(ctx_peers) + len(exp_peers))


class Gather:
    def __init__(self, own, out, send_sem, recv_sem, local_sem):
        me = lax.axis_index("ctx")
        sib, across, along = ctx_neighbours(me)
        half = own.shape[0] // 2
        first, second = pl.ds(0, half), pl.ds(half, half)
        far = ctx_neighbours(across)[2]

        def copy(k, source, target, peer):
            return pltpu.make_async_remote_copy(
                src_ref=source,
                dst_ref=target,
                send_sem=send_sem.at[k],
                recv_sem=recv_sem.at[k],
                device_id={"ctx": peer},
                device_id_type=MESH,
            )

        self.local = pltpu.make_async_copy(own, out.at[me], local_sem)
        self.c = [
            copy(0, own.at[first], out.at[me, first], across),
            copy(1, own.at[second], out.at[me, second], along),
            copy(2, own.at[second], out.at[me, second], across),
            copy(3, own.at[first], out.at[me, first], along),
            copy(4, own, out.at[me], sib),
            copy(5, out.at[across, first], out.at[across, first], along),
            copy(6, out.at[along, second], out.at[along, second], across),
            copy(7, out.at[across], out.at[across], sib),
            copy(8, out.at[along], out.at[along], sib),
            copy(9, out.at[far, first], out.at[far, first], sib),
            copy(10, out.at[far, second], out.at[far, second], sib),
        ]

    def start_first(self):
        self.c[0].start()
        self.c[1].start()

    def start_rest(self):
        self.c[2].start()
        self.c[3].start()
        self.c[4].start()
        self.local.start()

    def relay(self):
        self.c[0].wait_recv()
        self.c[5].start()
        self.c[1].wait_recv()
        self.c[6].start()

    def share_near(self):
        self.c[2].wait_recv()
        self.c[7].start()
        self.c[3].wait_recv()
        self.c[8].start()

    def share_far(self):
        self.c[5].wait_recv()
        self.c[9].start()
        self.c[6].wait_recv()
        self.c[10].start()

    def finish(self):
        for k in (4, 7, 8, 9, 10):
            self.c[k].wait_recv()
        for one in self.c:
            one.wait_send()
        self.local.wait()


def dispatch_kernel(
    n_exp, cap,
    tok, cot, ids_row, ids_col, weight_col, w_gate, w_up, w_down,
    x_out, y_out, gate_out, up_out, down_out, table_out,
    send_x, send_y, g_send, g_recv, g_local, d_send, d_recv, d_local,
):
    me_exp = lax.axis_index("exp")
    me = lax.axis_index("ctx")
    exp_peers = [lax.rem(me_exp + d, n_exp) for d in range(1, n_exp)]
    enter(list(ctx_neighbours(me)), exp_peers)
    gathers = [
        Gather(own.at[0], out, g_send.at[i], g_recv.at[i], g_local.at[i])
        for i, (own, out) in enumerate(((w_down, down_out), (w_gate, gate_out), (w_up, up_out)))
    ]
    for g in gathers:
        g.start_first()
    for g in gathers:
        g.start_rest()
    count = tok.shape[0]
    row = ids_row[...]
    same = ids_col[...] == row
    before = lax.broadcasted_iota(jnp.int32, (count, count), 0) < lax.broadcasted_iota(
        jnp.int32, (count, count), 1
    )
    position = jnp.sum(jnp.where(same & before, 1.0, 0.0), axis=0, keepdims=True)
    target = row * cap + position.astype(jnp.int32)
    scaled = (weight_col[...] * cot[...].astype(jnp.float32)).astype(jnp.bfloat16)
    for k in range(n_exp):
        places = lax.broadcasted_iota(jnp.int32, (cap, count), 0) + k * cap
        table = jnp.where(places == target, 1.0, 0.0).astype(jnp.bfloat16)
        table_out[pl.ds(k * cap, cap), :] = table
        send_x[k] = jnp.dot(table, tok[...], preferred_element_type=jnp.float32).astype(jnp.bfloat16)
        send_y[k] = jnp.dot(table, scaled, preferred_element_type=jnp.float32).astype(jnp.bfloat16)
    copies = []
    for d, peer in enumerate(exp_peers):
        for which, (source, out) in enumerate(((send_x, x_out), (send_y, y_out))):
            copies.append(
                pltpu.make_async_remote_copy(
                    src_ref=source.at[peer],
                    dst_ref=out.at[me_exp],
                    send_sem=d_send.at[d, which],
                    recv_sem=d_recv.at[d, which],
                    device_id={"exp": peer},
                    device_id_type=MESH,
                )
            )
    for one in copies:
        one.start()
    kept = [
        pltpu.make_async_copy(send_x.at[me_exp], x_out.at[me_exp], d_local.at[0]),
        pltpu.make_async_copy(send_y.at[me_exp], y_out.at[me_exp], d_local.at[1]),
    ]
    for one in kept:
        one.start()
    for g in gathers:
        g.relay()
    for g in gathers:
        g.share_near()
    for g in gathers:
        g.share_far()
    for one in copies + kept:
        one.wait()
    for g in gathers:
        g.finish()


def return_kernel(
    n_exp, n_ctx,
    hidden, d_gate, d_up, x_rows, y_rows, back, inner,
    hidden_out, gate_out, up_out, x_out, y_out, back_out, inner_out,
    g_send, g_recv, g_local, x_send, x_recv, x_local, d_send, d_recv, d_local,
):
    me_exp = lax.axis_index("exp")
    me = lax.axis_index("ctx")
    exp_peers = [lax.rem(me_exp + d, n_exp) for d in range(1, n_exp)]
    ctx_peers = [lax.rem(me + d, n_ctx) for d in range(1, n_ctx)]
    enter(ctx_peers, exp_peers)
    gathers = [
        Gather(own, out, g_send.at[i], g_recv.at[i], g_local.at[i])
        for i, (own, out) in enumerate(((hidden, hidden_out), (d_gate, gate_out), (d_up, up_out)))
    ]
    for g in gathers:
        g.start_first()
    copies = []
    for d, peer in enumerate(exp_peers):
        for which, (source, out) in enumerate(((back, back_out), (inner, inner_out))):
            copies.append(
                pltpu.make_async_remote_copy(
                    src_ref=source.at[peer],
                    dst_ref=out.at[me_exp],
                    send_sem=d_send.at[d, which],
                    recv_sem=d_recv.at[d, which],
                    device_id={"exp": peer},
                    device_id_type=MESH,
                )
            )
    width = x_out.shape[2]

    def columns(at):
        return pl.ds(pl.multiple_of(at * width, width), width)

    for one in copies:
        one.start()
    for g in gathers:
        g.start_rest()
    moves = []
    for d, peer in enumerate(ctx_peers):
        for which, (source, out) in enumerate(((x_rows, x_out), (y_rows, y_out))):
            moves.append(
                pltpu.make_async_remote_copy(
                    src_ref=source.at[:, columns(peer)],
                    dst_ref=out.at[me],
                    send_sem=x_send.at[d, which],
                    recv_sem=x_recv.at[d, which],
                    device_id={"ctx": peer},
                    device_id_type=MESH,
                )
            )
    for one in moves:
        one.start()
    kept = [
        pltpu.make_async_copy(back.at[me_exp], back_out.at[me_exp], d_local.at[0]),
        pltpu.make_async_copy(inner.at[me_exp], inner_out.at[me_exp], d_local.at[1]),
        pltpu.make_async_copy(x_rows.at[:, columns(me)], x_out.at[me], x_local.at[0]),
        pltpu.make_async_copy(y_rows.at[:, columns(me)], y_out.at[me], x_local.at[1]),
    ]
    for one in kept:
        one.start()
    for g in gathers:
        g.relay()
    for g in gathers:
        g.share_near()
    for g in gathers:
        g.share_far()
    for one in copies + moves + kept:
        one.wait()
    for g in gathers:
        g.finish()


def fast_body(tokens, cotangent, expert_ids, route_weights, w_gate, w_up, w_down):
    n_ctx = lax.axis_size("ctx")
    n_exp = lax.axis_size("exp")
    count, width = tokens.shape
    cap = max(2, (3 * count + 2 * n_exp - 1) // (2 * n_exp))
    cols = width // n_ctx
    units = w_gate.shape[2]
    rows = n_exp * cap
    bf = jnp.bfloat16
    vm = pl.BlockSpec(memory_space=pltpu.VMEM)
    hbm = pl.BlockSpec(memory_space=pl.ANY)
    dma = pltpu.SemaphoreType.DMA
    x, y, gate_w, up_w, down_w, table = pl.pallas_call(
        functools.partial(dispatch_kernel, n_exp, cap),
        out_shape=(
            jax.ShapeDtypeStruct((n_exp, cap, width), bf),
            jax.ShapeDtypeStruct((n_exp, cap, width), bf),
            jax.ShapeDtypeStruct((n_ctx, cols, units), bf),
            jax.ShapeDtypeStruct((n_ctx, cols, units), bf),
            jax.ShapeDtypeStruct((n_ctx, units, cols), bf),
            jax.ShapeDtypeStruct((rows, count), bf),
        ),
        in_specs=[vm] * 5 + [hbm] * 3,
        out_specs=(hbm,) * 5 + (vm,),
        scratch_shapes=[
            pltpu.VMEM((n_exp, cap, width), bf),
            pltpu.VMEM((n_exp, cap, width), bf),
            dma((3, 11)), dma((3, 11)), dma((3,)),
            dma((n_exp - 1, 2)), dma((n_exp - 1, 2)), dma((2,)),
        ],
        compiler_params=pltpu.CompilerParams(collective_id=0, has_side_effects=True),
    )(
        tokens, cotangent, expert_ids.reshape(1, count), expert_ids.reshape(count, 1),
        route_weights.reshape(count, 1), w_gate, w_up, w_down,
    )
    x = x.reshape(rows, width)
    y = y.reshape(rows, width)
    f32 = jnp.float32
    gate_flat = gate_w.reshape(width, units)
    up_flat = up_w.reshape(width, units)
    gate = jnp.dot(x, gate_flat, preferred_element_type=f32)
    up = jnp.dot(x, up_flat, preferred_element_type=f32)
    back_sum = jnp.zeros((rows, units), f32)
    for c in range(n_ctx):
        back_sum = back_sum + lax.dot_general(
            y[:, c * cols:(c + 1) * cols], down_w[c], (((1,), (1,)), ((), ())),
            preferred_element_type=f32,
        )
    sig = jax.nn.sigmoid(gate)
    hidden = (gate * sig * up).astype(bf)
    d_up = (back_sum * gate * sig).astype(bf)
    d_gate = (back_sum * up * sig * (1.0 + gate * (1.0 - sig))).astype(bf)
    inner = jnp.sum(hidden.astype(f32) * back_sum, axis=1)
    inner = jnp.broadcast_to(
        jnp.pad(inner.reshape(n_exp, 1, cap), ((0, 0), (0, 0), (0, 128 - cap))), (n_exp, 8, 128)
    )
    last = (((1,), (1,)), ((), ()))
    back = (
        lax.dot_general(d_gate, gate_flat, last, preferred_element_type=f32)
        + lax.dot_general(d_up, up_flat, last, preferred_element_type=f32)
    ).astype(bf).reshape(n_exp, cap, width)
    hid_all, dg_all, du_all, x_all, y_all, home, home_inner = pl.pallas_call(
        functools.partial(return_kernel, n_exp, n_ctx),
        out_shape=(
            jax.ShapeDtypeStruct((n_ctx, rows, units), bf),
            jax.ShapeDtypeStruct((n_ctx, rows, units), bf),
            jax.ShapeDtypeStruct((n_ctx, rows, units), bf),
            jax.ShapeDtypeStruct((n_ctx, rows, cols), bf),
            jax.ShapeDtypeStruct((n_ctx, rows, cols), bf),
            jax.ShapeDtypeStruct((n_exp, cap, width), bf),
            jax.ShapeDtypeStruct((n_exp, 8, 128), f32),
        ),
        in_specs=[hbm] * 7,
        out_specs=(hbm,) * 7,
        scratch_shapes=[
            dma((3, 11)), dma((3, 11)), dma((3,)),
            dma((n_ctx - 1, 2)), dma((n_ctx - 1, 2)), dma((2,)),
            dma((n_exp - 1, 2)), dma((n_exp - 1, 2)), dma((2,)),
        ],
        compiler_params=pltpu.CompilerParams(collective_id=1, has_side_effects=True),
    )(hidden, d_gate, d_up, x, y, back, inner)
    first = (((0,), (0,)), ((), ()))
    total = n_ctx * rows

    def over_rows(a, b):
        return lax.dot_general(
            a.reshape(total, -1), b.reshape(total, -1), first, preferred_element_type=f32
        ).astype(bf)[None]

    gate_grads = over_rows(x_all, dg_all)
    up_grads = over_rows(x_all, du_all)
    down_grads = over_rows(hid_all, y_all)
    token_grads = lax.dot_general(
        table, home.reshape(rows, width), first, preferred_element_type=f32
    ).astype(bf)
    flat = home_inner[:, 0, :cap].reshape(rows, 1)
    route = jnp.sum(table.astype(f32) * flat, axis=0).reshape(count, 1)
    return (token_grads, route / route_weights, gate_grads, up_grads, down_grads)


def solution(mesh):
    return jax.shard_map(
        fast_body if mesh.shape["ctx"] == 8 else body,
        mesh=mesh,
        in_specs=(
            P(("ctx", "exp"), None),
            P(("ctx", "exp"), None),
            P(("ctx", "exp"), None),
            P(("ctx", "exp"), None),
            P("exp", "ctx", None),
            P("exp", "ctx", None),
            P("exp", None, "ctx"),
        ),
        out_specs=(
            P(("ctx", "exp"), None),
            P(("ctx", "exp"), None),
            P("exp", "ctx", None),
            P("exp", "ctx", None),
            P("exp", None, "ctx"),
        ),
        check_vma=False,
    )
```

```python
import functools

import jax
import jax.numpy as jnp
from jax import lax
from jax.experimental import pallas as pl
from jax.experimental.pallas import tpu as pltpu
from jax.sharding import PartitionSpec as P

MESH = pl.DeviceIdType.MESH


def slot_table(route_ids, expert_count, capacity):
    labels = jnp.arange(expert_count, dtype=jnp.int32)
    onehot = (route_ids[..., :, None] == labels).astype(jnp.int32)
    position = jnp.sum((jnp.cumsum(onehot, axis=-2) - 1) * onehot, axis=-1)
    target = route_ids * capacity + position
    places = jnp.arange(expert_count * capacity, dtype=jnp.int32)
    return (target[..., None, :] == places[:, None]).astype(jnp.bfloat16)


def forward_hidden(totals, units):
    gate_pre = totals[:, :units]
    up_pre = totals[:, units:]
    gate_sig = jax.nn.sigmoid(gate_pre)
    return (gate_pre * gate_sig * up_pre).astype(jnp.bfloat16)


def backward_grads(totals, back_sum, units):
    gate_pre = totals[:, :units]
    up_pre = totals[:, units:]
    gate_sig = jax.nn.sigmoid(gate_pre)
    d_up = (back_sum * gate_pre * gate_sig).astype(jnp.bfloat16)
    d_gate = (back_sum * up_pre * gate_sig * (1.0 + gate_pre * (1.0 - gate_sig))).astype(
        jnp.bfloat16
    )
    return jnp.concatenate([d_gate, d_up], axis=1)


def body(tokens, cotangent, expert_ids, route_weights, w_gate, w_up, w_down):
    ctx_size = lax.axis_size("ctx")
    exp_size = lax.axis_size("exp")
    tok_count, model_width = tokens.shape
    route_count = expert_ids.shape[1]
    slot_count = tok_count * route_count
    expert_count = w_gate.shape[0] * exp_size
    capacity = max(2, (3 * slot_count + 2 * expert_count - 1) // (2 * expert_count))
    col_count = model_width // ctx_size
    units = w_gate.shape[2]
    row_count = ctx_size * exp_size * capacity
    own_rows = row_count // ctx_size
    all_ids = lax.all_gather(expert_ids, "ctx", axis=0, tiled=True)
    tables = slot_table(all_ids.reshape(ctx_size, slot_count), expert_count, capacity)
    token_slots = jnp.repeat(tokens, route_count, axis=0)
    scaled = (
        route_weights * jnp.repeat(cotangent, route_count, axis=0).astype(jnp.float32)
    ).astype(jnp.bfloat16)
    own_table = lax.dynamic_index_in_dim(tables, lax.axis_index("ctx"), 0, keepdims=False)
    send_x = jnp.dot(own_table, token_slots, preferred_element_type=jnp.float32).astype(
        jnp.bfloat16
    )
    send_y = jnp.dot(own_table, scaled, preferred_element_type=jnp.float32).astype(jnp.bfloat16)
    send_x = send_x.reshape(expert_count, capacity, model_width)
    send_y = send_y.reshape(expert_count, capacity, model_width)
    group_x, group_y = (
        lax.all_to_all(send_x, "exp", split_axis=0, concat_axis=0, tiled=True),
        lax.all_to_all(send_y, "exp", split_axis=0, concat_axis=0, tiled=True),
    )
    slot_x, slot_y = (
        lax.all_to_all(group_x, "ctx", split_axis=2, concat_axis=0, tiled=True),
        lax.all_to_all(group_y, "ctx", split_axis=2, concat_axis=0, tiled=True),
    )
    slot_x = slot_x.reshape(row_count, col_count)
    slot_y = slot_y.reshape(row_count, col_count)
    gate_weight = w_gate[0]
    up_weight = w_up[0]
    down_weight = w_down[0]
    both_weights = jnp.concatenate([gate_weight, up_weight], axis=1)

    def fold_grad(segment):
        gate_acc = lax.dot_general(
            slot_x, segment[:, :units], (((0,), (0,)), ((), ())), preferred_element_type=jnp.float32
        )
        up_acc = lax.dot_general(
            slot_x, segment[:, units:], (((0,), (0,)), ((), ())), preferred_element_type=jnp.float32
        )
        grad_rows = lax.dot_general(
            segment, both_weights, (((1,), (1,)), ((), ())), preferred_element_type=jnp.float32
        )
        return (gate_acc, up_acc, grad_rows)

    row_x, row_y = (
        lax.all_to_all(slot_x, "ctx", split_axis=0, concat_axis=1, tiled=True),
        lax.all_to_all(slot_y, "ctx", split_axis=0, concat_axis=1, tiled=True),
    )
    full_gate, full_up, full_down = (
        lax.all_gather(gate_weight, "ctx", axis=0, tiled=True),
        lax.all_gather(up_weight, "ctx", axis=0, tiled=True),
        lax.all_gather(down_weight, "ctx", axis=1, tiled=True),
    )
    full_both = jnp.concatenate([full_gate, full_up], axis=1).reshape(
        ctx_size, col_count, 2 * units
    )
    gate_blocks = jnp.einsum(
        "rcd,cdf->crf",
        row_x.reshape(own_rows, ctx_size, col_count),
        full_both,
        preferred_element_type=jnp.float32,
    ).astype(jnp.bfloat16)
    totals_own = jnp.sum(gate_blocks.astype(jnp.float32), axis=0)
    hidden_own = forward_hidden(totals_own, units)
    back_blocks = jnp.einsum(
        "rcd,fcd->crf",
        row_y.reshape(own_rows, ctx_size, col_count),
        full_down.reshape(units, ctx_size, col_count),
        preferred_element_type=jnp.float32,
    ).astype(jnp.bfloat16)
    back_own = jnp.sum(back_blocks.astype(jnp.float32), axis=0)
    grads_own = backward_grads(totals_own, back_own, units)
    segment = (
        lax.all_gather(hidden_own, "ctx", axis=0, tiled=True),
        lax.all_gather(grads_own, "ctx", axis=0, tiled=True),
    )
    fold_segment = segment[0]
    outputs = jnp.dot(fold_segment, down_weight, preferred_element_type=jnp.float32)
    inner_rows = jnp.sum(slot_y.astype(jnp.float32) * outputs, axis=1)
    inner_all = inner_rows
    down_acc = lax.dot_general(
        fold_segment, slot_y, (((0,), (0,)), ((), ())), preferred_element_type=jnp.float32
    )
    down_state = (down_acc, inner_all)
    grad_state = fold_grad(segment[1])
    down_acc = down_state[0]
    inner_all = down_state[1]
    gate_acc = grad_state[0]
    up_acc = grad_state[1]
    back_rows = grad_state[2]
    back_slots = back_rows.astype(jnp.bfloat16).reshape(ctx_size, exp_size, capacity, col_count)
    inner_slots = inner_all.reshape(ctx_size, exp_size, capacity)
    home_back = lax.all_to_all(back_slots, "exp", split_axis=1, concat_axis=1, tiled=True)
    home_inner = lax.all_to_all(inner_slots, "exp", split_axis=1, concat_axis=1, tiled=True)
    merged = jnp.einsum(
        "cks,ckd->csd",
        tables,
        home_back.reshape(ctx_size, expert_count * capacity, col_count),
        preferred_element_type=jnp.float32,
    )
    merged = jnp.sum(merged.reshape(ctx_size, tok_count, route_count, col_count), axis=2).astype(
        jnp.bfloat16
    )
    grads_home = lax.all_to_all(merged, "ctx", split_axis=0, concat_axis=2, tiled=True)
    token_grads = grads_home.reshape(tok_count, model_width)
    inner_home = jnp.einsum(
        "cks,ck->cs",
        tables.astype(jnp.float32),
        home_inner.reshape(ctx_size, expert_count * capacity),
        precision=lax.Precision.HIGHEST,
    )
    route_sums = lax.psum_scatter(inner_home, "ctx", scatter_dimension=0, tiled=True).reshape(
        tok_count, route_count
    )
    route_grads = route_sums / route_weights
    gate_grads = gate_acc.astype(jnp.bfloat16)[None]
    up_grads = up_acc.astype(jnp.bfloat16)[None]
    down_grads = down_acc.astype(jnp.bfloat16)[None]
    return (token_grads, route_grads, gate_grads, up_grads, down_grads)


def ctx_neighbours(me):
    sib = me + 1 - 2 * (me % 2)
    across = me + 2 - 4 * ((me // 2) % 2)
    along = me + 4 - 8 * ((me // 4) % 2)
    return sib, across, along


def enter(ctx_peers, exp_peers):
    barrier = pltpu.get_barrier_semaphore()
    for peer in ctx_peers:
        pl.semaphore_signal(barrier, inc=1, device_id={"ctx": peer}, device_id_type=MESH)
    for peer in exp_peers:
        pl.semaphore_signal(barrier, inc=1, device_id={"exp": peer}, device_id_type=MESH)
    pl.semaphore_wait(barrier, len(ctx_peers) + len(exp_peers))


class Gather:
    def __init__(self, own, out, send_sem, recv_sem):
        me = lax.axis_index("ctx")
        sib, across, along = ctx_neighbours(me)
        half = own.shape[0] // 2
        first, second = pl.ds(0, half), pl.ds(half, half)
        far = ctx_neighbours(across)[2]

        def copy(k, source, target, peer):
            return pltpu.make_async_remote_copy(
                src_ref=source,
                dst_ref=target,
                send_sem=send_sem.at[k],
                recv_sem=recv_sem.at[k],
                device_id={"ctx": peer},
                device_id_type=MESH,
            )

        self.c = [
            copy(0, own.at[first], out.at[me, first], across),
            copy(1, own.at[second], out.at[me, second], along),
            copy(2, own.at[second], out.at[me, second], across),
            copy(3, own.at[first], out.at[me, first], along),
            copy(4, own, out.at[me], sib),
            copy(5, out.at[across, first], out.at[across, first], along),
            copy(6, out.at[along, second], out.at[along, second], across),
            copy(7, out.at[across], out.at[across], sib),
            copy(8, out.at[along], out.at[along], sib),
            copy(9, out.at[far, first], out.at[far, first], sib),
            copy(10, out.at[far, second], out.at[far, second], sib),
        ]

    def start(self, *which):
        for k in which:
            self.c[k].start()

    def arrived(self, *which):
        for k in which:
            self.c[k].wait_recv()

    def relay(self):
        self.arrived(0)
        self.start(5)
        self.arrived(1)
        self.start(6)

    def share_near(self):
        self.arrived(2)
        self.start(7)
        self.arrived(3)
        self.start(8)

    def share_far(self):
        self.arrived(5)
        self.start(9)
        self.arrived(6)
        self.start(10)

    def sent(self):
        for one in self.c:
            one.wait_send()


NT = (((1,), (1,)), ((), ()))
TN = (((0,), (0,)), ((), ()))


def dot(a, b, dims):
    return lax.dot_general(a, b, dims, preferred_element_type=jnp.float32)


def kernel(
    n_exp, n_ctx, cap,
    tok, cot, ids_row, weight_row, w_gate, w_up, w_down,
    token_out, route_out, gate_grad, up_grad, down_grad,
    send_x, send_y, x_rows, y_rows, gate_w, up_w, down_w, table,
    gate_acc, up_acc, back_acc, hid_all, dg_all, du_all, x_all, y_all,
    back, inner, home, home_inner, gg_acc, ug_acc, dn_acc,
    w_send, w_recv, w_local, d_send, d_recv, d_local,
    s_send, s_recv, m_send, m_recv, m_local, r_send, r_recv, r_local,
):
    me_exp = lax.axis_index("exp")
    me = lax.axis_index("ctx")
    bf, f32 = jnp.bfloat16, jnp.float32
    sib, across, along = ctx_neighbours(me)
    far = ctx_neighbours(across)[2]
    exp_peers = [lax.rem(me_exp + d, n_exp) for d in range(1, n_exp)]
    ctx_peers = [lax.rem(me + d, n_ctx) for d in range(1, n_ctx)]
    enter(ctx_peers, exp_peers)

    weights = [
        Gather(own.at[0], out, w_send.at[i], w_recv.at[i])
        for i, (own, out) in enumerate(((w_gate, gate_w), (w_up, up_w), (w_down, down_w)))
    ]
    own_weights = [
        pltpu.make_async_copy(own.at[0], out.at[me], w_local.at[i])
        for i, (own, out) in enumerate(((w_gate, gate_w), (w_up, up_w), (w_down, down_w)))
    ]
    for g in weights:
        g.start(0, 1)
    for g in weights:
        g.start(2, 3)

    count, width = tok.shape
    cols = width // n_ctx

    def rows_of(at):
        return pl.ds(pl.multiple_of(at * cap, cap), cap)

    def columns(at):
        return pl.ds(pl.multiple_of(at * cols, cols), cols)

    down_i = lax.broadcasted_iota(jnp.int32, (count, count), 0)
    over_i = lax.broadcasted_iota(jnp.int32, (count, count), 1)
    row = ids_row[...]
    diagonal = down_i == over_i
    row_f = row.astype(f32)
    col_f = jnp.sum(jnp.where(diagonal, row_f, 0.0), axis=1, keepdims=True)
    weight_col = jnp.sum(jnp.where(diagonal, weight_row[...], 0.0), axis=1, keepdims=True)
    position = jnp.sum(
        jnp.where((col_f == row_f) & (down_i < over_i), 1.0, 0.0), axis=0, keepdims=True
    )
    target = row * cap + position.astype(jnp.int32)
    places = lax.broadcasted_iota(jnp.int32, (n_exp * cap, count), 0)
    table[...] = jnp.where(places == target, 1.0, 0.0).astype(bf)

    def exchange(source, out, sends, recvs, local, which):
        moves = [
            pltpu.make_async_remote_copy(
                src_ref=source.at[rows_of(peer)],
                dst_ref=out.at[rows_of(me_exp)],
                send_sem=sends.at[d, which],
                recv_sem=recvs.at[d, which],
                device_id={"exp": peer},
                device_id_type=MESH,
            )
            for d, peer in enumerate(exp_peers)
        ]
        moves.append(
            pltpu.make_async_copy(
                source.at[rows_of(me_exp)], out.at[rows_of(me_exp)], local.at[which]
            )
        )
        for one in moves:
            one.start()
        return moves

    send_x[...] = dot(table[...], tok[...], (((1,), (0,)), ((), ()))).astype(bf)
    sent_x = exchange(send_x, x_rows, d_send, d_recv, d_local, 0)
    scaled = (weight_col * cot[...].astype(f32)).astype(bf)
    send_y[...] = dot(table[...], scaled, (((1,), (0,)), ((), ()))).astype(bf)
    sent_y = exchange(send_y, y_rows, d_send, d_recv, d_local, 1)
    for g, one in zip(weights, own_weights):
        g.start(4)
        one.start()
    for g in weights:
        g.relay()
    for g in weights:
        g.share_near()

    def spread(source, out, which):
        moves = [
            pltpu.make_async_remote_copy(
                src_ref=source.at[:, columns(peer)],
                dst_ref=out.at[me],
                send_sem=m_send.at[d, which],
                recv_sem=m_recv.at[d, which],
                device_id={"ctx": peer},
                device_id_type=MESH,
            )
            for d, peer in enumerate(ctx_peers)
        ]
        moves.append(
            pltpu.make_async_copy(source.at[:, columns(me)], out.at[me], m_local.at[which])
        )
        for one in moves:
            one.start()
        return moves

    for g in weights:
        g.share_far()
    for one in sent_x:
        one.wait()
    moved = spread(x_rows, x_all, 0)
    for one in sent_y:
        one.wait()
    moved = moved + spread(y_rows, y_all, 1)

    def forward(c, start):
        xc = x_rows[:, columns(c)]
        yc = y_rows[:, columns(c)]
        parts = (
            dot(xc, gate_w[c], (((1,), (0,)), ((), ()))),
            dot(xc, up_w[c], (((1,), (0,)), ((), ()))),
            dot(yc, down_w[c], NT),
        )
        for acc, part in zip((gate_acc, up_acc, back_acc), parts):
            acc[...] = part if start else acc[...] + part

    for one in own_weights:
        one.wait()
    forward(me, True)
    for g in weights:
        g.arrived(4)
    forward(sib, False)
    forward(across, False)
    forward(along, False)
    forward(far, False)
    for g in weights:
        g.arrived(7, 8)
    forward(ctx_neighbours(across)[0], False)
    forward(ctx_neighbours(along)[0], False)
    for g in weights:
        g.arrived(9, 10)
    forward(ctx_neighbours(far)[0], False)

    gate, up, back_sum = gate_acc[...], up_acc[...], back_acc[...]
    sig = 1.0 / (1.0 + jnp.exp(-gate))
    hidden = (gate * sig * up).astype(bf)
    hid_all[me] = hidden
    dg_all[me] = (back_sum * up * sig * (1.0 + gate * (1.0 - sig))).astype(bf)
    du_all[me] = (back_sum * gate * sig).astype(bf)
    states = [
        Gather(out.at[me], out, s_send.at[i], s_recv.at[i])
        for i, out in enumerate((hid_all, dg_all, du_all))
    ]
    for g in states:
        g.start(0, 1)
    for g in states:
        g.start(2, 3)
    for g in states:
        g.start(4)
    inner[...] = jnp.broadcast_to(
        jnp.sum(hidden.astype(f32) * back_sum, axis=1, keepdims=True), inner.shape
    )
    sent_inner = exchange(inner, home_inner, r_send, r_recv, r_local, 0)
    for c in range(n_ctx):
        back[:, c * cols:(c + 1) * cols] = (
            dot(dg_all[me], gate_w[c], NT) + dot(du_all[me], up_w[c], NT)
        ).astype(bf)
    sent_back = exchange(back, home, r_send, r_recv, r_local, 1)
    for g in states:
        g.relay()
    for g in states:
        g.share_near()
    for one in moved:
        one.wait()

    def fold(c, start):
        xc, yc = x_all[c], y_all[c]
        parts = (dot(yc, hid_all[c], TN), dot(xc, dg_all[c], TN), dot(xc, du_all[c], TN))
        for acc, part in zip((dn_acc, gg_acc, ug_acc), parts):
            acc[...] = part if start else acc[...] + part

    fold(me, True)
    for g in states:
        g.arrived(4)
    fold(sib, False)
    for g in states:
        g.share_far()
    fold(across, False)
    fold(along, False)
    for one in sent_inner + sent_back:
        one.wait()
    token_out[...] = dot(table[...], home[...], TN).astype(bf)
    route_out[...] = (
        jnp.sum(table[...].astype(f32) * home_inner[...], axis=0, keepdims=True) / weight_row[...]
    )
    fold(far, False)
    for g in states:
        g.arrived(7, 8)
    fold(ctx_neighbours(across)[0], False)
    fold(ctx_neighbours(along)[0], False)
    for g in states:
        g.arrived(9, 10)
    fold(ctx_neighbours(far)[0], False)
    gate_grad[...] = gg_acc[...].astype(bf)
    up_grad[...] = ug_acc[...].astype(bf)
    down_grad[...] = dn_acc[...].T.astype(bf)
    for g in weights + states:
        g.sent()


def fast_body(tokens, cotangent, expert_ids, route_weights, w_gate, w_up, w_down):
    n_ctx = lax.axis_size("ctx")
    n_exp = lax.axis_size("exp")
    count, width = tokens.shape
    cap = max(2, (3 * count + 2 * n_exp - 1) // (2 * n_exp))
    cols = width // n_ctx
    units = w_gate.shape[2]
    rows = n_exp * cap
    bf, f32 = jnp.bfloat16, jnp.float32
    vm = pl.BlockSpec(memory_space=pltpu.VMEM)
    hbm = pl.BlockSpec(memory_space=pl.ANY)
    dma = pltpu.SemaphoreType.DMA
    token_grads, route, gate_grads, up_grads, down_grads = pl.pallas_call(
        functools.partial(kernel, n_exp, n_ctx, cap),
        out_shape=(
            jax.ShapeDtypeStruct((count, width), bf),
            jax.ShapeDtypeStruct((1, count), f32),
            jax.ShapeDtypeStruct((cols, units), bf),
            jax.ShapeDtypeStruct((cols, units), bf),
            jax.ShapeDtypeStruct((units, cols), bf),
        ),
        in_specs=[vm] * 4 + [hbm] * 3,
        out_specs=(vm,) * 5,
        scratch_shapes=[pltpu.VMEM((rows, width), bf)] * 4
        + [
            pltpu.VMEM((n_ctx, cols, units), bf),
            pltpu.VMEM((n_ctx, cols, units), bf),
            pltpu.VMEM((n_ctx, units, cols), bf),
            pltpu.VMEM((rows, count), bf),
        ]
        + [pltpu.VMEM((rows, units), f32)] * 3
        + [pltpu.VMEM((n_ctx, rows, units), bf)] * 3
        + [pltpu.VMEM((n_ctx, rows, cols), bf)] * 2
        + [
            pltpu.VMEM((rows, width), bf),
            pltpu.VMEM((rows, count), f32),
            pltpu.VMEM((rows, width), bf),
            pltpu.VMEM((rows, count), f32),
        ]
        + [pltpu.VMEM((cols, units), f32)] * 3
        + [
            dma((3, 11)), dma((3, 11)), dma((3,)),
            dma((n_exp - 1, 2)), dma((n_exp - 1, 2)), dma((2,)),
            dma((3, 11)), dma((3, 11)),
            dma((n_ctx - 1, 2)), dma((n_ctx - 1, 2)), dma((2,)),
            dma((n_exp - 1, 2)), dma((n_exp - 1, 2)), dma((2,)),
        ],
        compiler_params=pltpu.CompilerParams(
            collective_id=0, has_side_effects=True, vmem_limit_bytes=56 * 1024 * 1024
        ),
    )(
        tokens, cotangent, expert_ids.reshape(1, count), route_weights.reshape(1, count),
        w_gate, w_up, w_down,
    )
    return (
        token_grads, route.reshape(count, 1), gate_grads[None], up_grads[None], down_grads[None]
    )


def solution(mesh):
    return jax.shard_map(
        fast_body if mesh.shape["ctx"] == 8 else body,
        mesh=mesh,
        in_specs=(
            P(("ctx", "exp"), None),
            P(("ctx", "exp"), None),
            P(("ctx", "exp"), None),
            P(("ctx", "exp"), None),
            P("exp", "ctx", None),
            P("exp", "ctx", None),
            P("exp", None, "ctx"),
        ),
        out_specs=(
            P(("ctx", "exp"), None),
            P(("ctx", "exp"), None),
            P("exp", "ctx", None),
            P("exp", "ctx", None),
            P("exp", None, "ctx"),
        ),
        check_vma=False,
    )
```

```python
import functools

import jax
import jax.numpy as jnp
from jax import lax
from jax.experimental import pallas as pl
from jax.experimental.pallas import tpu as pltpu
from jax.sharding import PartitionSpec as P

MESH = pl.DeviceIdType.MESH


def slot_table(route_ids, expert_count, capacity):
    labels = jnp.arange(expert_count, dtype=jnp.int32)
    onehot = (route_ids[..., :, None] == labels).astype(jnp.int32)
    position = jnp.sum((jnp.cumsum(onehot, axis=-2) - 1) * onehot, axis=-1)
    target = route_ids * capacity + position
    places = jnp.arange(expert_count * capacity, dtype=jnp.int32)
    return (target[..., None, :] == places[:, None]).astype(jnp.bfloat16)


def forward_hidden(totals, units):
    gate_pre = totals[:, :units]
    up_pre = totals[:, units:]
    gate_sig = jax.nn.sigmoid(gate_pre)
    return (gate_pre * gate_sig * up_pre).astype(jnp.bfloat16)


def backward_grads(totals, back_sum, units):
    gate_pre = totals[:, :units]
    up_pre = totals[:, units:]
    gate_sig = jax.nn.sigmoid(gate_pre)
    d_up = (back_sum * gate_pre * gate_sig).astype(jnp.bfloat16)
    d_gate = (back_sum * up_pre * gate_sig * (1.0 + gate_pre * (1.0 - gate_sig))).astype(
        jnp.bfloat16
    )
    return jnp.concatenate([d_gate, d_up], axis=1)


def body(tokens, cotangent, expert_ids, route_weights, w_gate, w_up, w_down):
    ctx_size = lax.axis_size("ctx")
    exp_size = lax.axis_size("exp")
    tok_count, model_width = tokens.shape
    route_count = expert_ids.shape[1]
    slot_count = tok_count * route_count
    expert_count = w_gate.shape[0] * exp_size
    capacity = max(2, (3 * slot_count + 2 * expert_count - 1) // (2 * expert_count))
    col_count = model_width // ctx_size
    units = w_gate.shape[2]
    row_count = ctx_size * exp_size * capacity
    own_rows = row_count // ctx_size
    all_ids = lax.all_gather(expert_ids, "ctx", axis=0, tiled=True)
    tables = slot_table(all_ids.reshape(ctx_size, slot_count), expert_count, capacity)
    token_slots = jnp.repeat(tokens, route_count, axis=0)
    scaled = (
        route_weights * jnp.repeat(cotangent, route_count, axis=0).astype(jnp.float32)
    ).astype(jnp.bfloat16)
    own_table = lax.dynamic_index_in_dim(tables, lax.axis_index("ctx"), 0, keepdims=False)
    send_x = jnp.dot(own_table, token_slots, preferred_element_type=jnp.float32).astype(
        jnp.bfloat16
    )
    send_y = jnp.dot(own_table, scaled, preferred_element_type=jnp.float32).astype(jnp.bfloat16)
    send_x = send_x.reshape(expert_count, capacity, model_width)
    send_y = send_y.reshape(expert_count, capacity, model_width)
    group_x, group_y = (
        lax.all_to_all(send_x, "exp", split_axis=0, concat_axis=0, tiled=True),
        lax.all_to_all(send_y, "exp", split_axis=0, concat_axis=0, tiled=True),
    )
    slot_x, slot_y = (
        lax.all_to_all(group_x, "ctx", split_axis=2, concat_axis=0, tiled=True),
        lax.all_to_all(group_y, "ctx", split_axis=2, concat_axis=0, tiled=True),
    )
    slot_x = slot_x.reshape(row_count, col_count)
    slot_y = slot_y.reshape(row_count, col_count)
    gate_weight = w_gate[0]
    up_weight = w_up[0]
    down_weight = w_down[0]
    both_weights = jnp.concatenate([gate_weight, up_weight], axis=1)

    def fold_grad(segment):
        gate_acc = lax.dot_general(
            slot_x, segment[:, :units], (((0,), (0,)), ((), ())), preferred_element_type=jnp.float32
        )
        up_acc = lax.dot_general(
            slot_x, segment[:, units:], (((0,), (0,)), ((), ())), preferred_element_type=jnp.float32
        )
        grad_rows = lax.dot_general(
            segment, both_weights, (((1,), (1,)), ((), ())), preferred_element_type=jnp.float32
        )
        return (gate_acc, up_acc, grad_rows)

    row_x, row_y = (
        lax.all_to_all(slot_x, "ctx", split_axis=0, concat_axis=1, tiled=True),
        lax.all_to_all(slot_y, "ctx", split_axis=0, concat_axis=1, tiled=True),
    )
    full_gate, full_up, full_down = (
        lax.all_gather(gate_weight, "ctx", axis=0, tiled=True),
        lax.all_gather(up_weight, "ctx", axis=0, tiled=True),
        lax.all_gather(down_weight, "ctx", axis=1, tiled=True),
    )
    full_both = jnp.concatenate([full_gate, full_up], axis=1).reshape(
        ctx_size, col_count, 2 * units
    )
    gate_blocks = jnp.einsum(
        "rcd,cdf->crf",
        row_x.reshape(own_rows, ctx_size, col_count),
        full_both,
        preferred_element_type=jnp.float32,
    ).astype(jnp.bfloat16)
    totals_own = jnp.sum(gate_blocks.astype(jnp.float32), axis=0)
    hidden_own = forward_hidden(totals_own, units)
    back_blocks = jnp.einsum(
        "rcd,fcd->crf",
        row_y.reshape(own_rows, ctx_size, col_count),
        full_down.reshape(units, ctx_size, col_count),
        preferred_element_type=jnp.float32,
    ).astype(jnp.bfloat16)
    back_own = jnp.sum(back_blocks.astype(jnp.float32), axis=0)
    grads_own = backward_grads(totals_own, back_own, units)
    segment = (
        lax.all_gather(hidden_own, "ctx", axis=0, tiled=True),
        lax.all_gather(grads_own, "ctx", axis=0, tiled=True),
    )
    fold_segment = segment[0]
    outputs = jnp.dot(fold_segment, down_weight, preferred_element_type=jnp.float32)
    inner_rows = jnp.sum(slot_y.astype(jnp.float32) * outputs, axis=1)
    inner_all = inner_rows
    down_acc = lax.dot_general(
        fold_segment, slot_y, (((0,), (0,)), ((), ())), preferred_element_type=jnp.float32
    )
    down_state = (down_acc, inner_all)
    grad_state = fold_grad(segment[1])
    down_acc = down_state[0]
    inner_all = down_state[1]
    gate_acc = grad_state[0]
    up_acc = grad_state[1]
    back_rows = grad_state[2]
    back_slots = back_rows.astype(jnp.bfloat16).reshape(ctx_size, exp_size, capacity, col_count)
    inner_slots = inner_all.reshape(ctx_size, exp_size, capacity)
    home_back = lax.all_to_all(back_slots, "exp", split_axis=1, concat_axis=1, tiled=True)
    home_inner = lax.all_to_all(inner_slots, "exp", split_axis=1, concat_axis=1, tiled=True)
    merged = jnp.einsum(
        "cks,ckd->csd",
        tables,
        home_back.reshape(ctx_size, expert_count * capacity, col_count),
        preferred_element_type=jnp.float32,
    )
    merged = jnp.sum(merged.reshape(ctx_size, tok_count, route_count, col_count), axis=2).astype(
        jnp.bfloat16
    )
    grads_home = lax.all_to_all(merged, "ctx", split_axis=0, concat_axis=2, tiled=True)
    token_grads = grads_home.reshape(tok_count, model_width)
    inner_home = jnp.einsum(
        "cks,ck->cs",
        tables.astype(jnp.float32),
        home_inner.reshape(ctx_size, expert_count * capacity),
        precision=lax.Precision.HIGHEST,
    )
    route_sums = lax.psum_scatter(inner_home, "ctx", scatter_dimension=0, tiled=True).reshape(
        tok_count, route_count
    )
    route_grads = route_sums / route_weights
    gate_grads = gate_acc.astype(jnp.bfloat16)[None]
    up_grads = up_acc.astype(jnp.bfloat16)[None]
    down_grads = down_acc.astype(jnp.bfloat16)[None]
    return (token_grads, route_grads, gate_grads, up_grads, down_grads)


def ctx_neighbours(me):
    sib = me + 1 - 2 * (me % 2)
    across = me + 2 - 4 * ((me // 2) % 2)
    along = me + 4 - 8 * ((me // 4) % 2)
    return sib, across, along


def enter(ctx_peers, exp_peers):
    barrier = pltpu.get_barrier_semaphore()
    for peer in ctx_peers:
        pl.semaphore_signal(barrier, inc=1, device_id={"ctx": peer}, device_id_type=MESH)
    for peer in exp_peers:
        pl.semaphore_signal(barrier, inc=1, device_id={"exp": peer}, device_id_type=MESH)
    pl.semaphore_wait(barrier, len(ctx_peers) + len(exp_peers))


class Gather:
    def __init__(self, own, out, send_sem, recv_sem):
        me = lax.axis_index("ctx")
        sib, across, along = ctx_neighbours(me)
        half = own.shape[0] // 2
        first, second = pl.ds(0, half), pl.ds(half, half)
        far = ctx_neighbours(across)[2]

        def copy(k, source, target, peer):
            return pltpu.make_async_remote_copy(
                src_ref=source,
                dst_ref=target,
                send_sem=send_sem.at[k],
                recv_sem=recv_sem.at[k],
                device_id={"ctx": peer},
                device_id_type=MESH,
            )

        self.c = [
            copy(0, own.at[first], out.at[me, first], across),
            copy(1, own.at[second], out.at[me, second], along),
            copy(2, own.at[second], out.at[me, second], across),
            copy(3, own.at[first], out.at[me, first], along),
            copy(4, own, out.at[me], sib),
            copy(5, out.at[across, first], out.at[across, first], along),
            copy(6, out.at[along, second], out.at[along, second], across),
            copy(7, out.at[across], out.at[across], sib),
            copy(8, out.at[along], out.at[along], sib),
            copy(9, out.at[far, first], out.at[far, first], sib),
            copy(10, out.at[far, second], out.at[far, second], sib),
        ]

    def start(self, *which):
        for k in which:
            self.c[k].start()

    def arrived(self, *which):
        for k in which:
            self.c[k].wait_recv()

    def relay(self):
        self.arrived(0)
        self.start(5)
        self.arrived(1)
        self.start(6)

    def share_near(self):
        self.arrived(2)
        self.start(7)
        self.arrived(3)
        self.start(8)

    def share_far(self):
        self.arrived(5)
        self.start(9)
        self.arrived(6)
        self.start(10)

    def sent(self):
        for one in self.c:
            one.wait_send()


NT = (((1,), (1,)), ((), ()))
TN = (((0,), (0,)), ((), ()))


def dot(a, b, dims):
    return lax.dot_general(a, b, dims, preferred_element_type=jnp.float32)


def kernel(
    n_exp, n_ctx, cap,
    tok, cot, ids_row, weight_row, w_gate, w_up, w_down,
    token_out, route_out, gate_grad, up_grad, down_grad,
    send_x, send_y, x_rows, y_rows, gate_w, up_w, down_w, table,
    gate_acc, up_acc, back_acc, hid_all, dg_all, du_all, x_all, y_all,
    back, inner, home, home_inner, gg_acc, ug_acc, dn_acc,
    w_send, w_recv, w_local, d_send, d_recv, d_local,
    s_send, s_recv, m_send, m_recv, m_local, r_send, r_recv, r_local,
):
    me_exp = lax.axis_index("exp")
    me = lax.axis_index("ctx")
    bf, f32 = jnp.bfloat16, jnp.float32
    sib, across, along = ctx_neighbours(me)
    far = ctx_neighbours(across)[2]
    exp_peers = [lax.rem(me_exp + d, n_exp) for d in range(1, n_exp)]
    ctx_peers = [lax.rem(me + d, n_ctx) for d in range(1, n_ctx)]
    enter(ctx_peers, exp_peers)

    weights = [
        Gather(own.at[0], out, w_send.at[i], w_recv.at[i])
        for i, (own, out) in enumerate(((w_gate, gate_w), (w_up, up_w), (w_down, down_w)))
    ]
    own_weights = [
        pltpu.make_async_copy(own.at[0], out.at[me], w_local.at[i])
        for i, (own, out) in enumerate(((w_gate, gate_w), (w_up, up_w), (w_down, down_w)))
    ]
    for g in weights:
        g.start(0, 1)
    for g in weights:
        g.start(2, 3)

    count, width = tok.shape
    cols = width // n_ctx

    def rows_of(at):
        return pl.ds(pl.multiple_of(at * cap, cap), cap)

    def columns(at):
        return pl.ds(pl.multiple_of(at * cols, cols), cols)

    down_i = lax.broadcasted_iota(jnp.int32, (count, count), 0)
    over_i = lax.broadcasted_iota(jnp.int32, (count, count), 1)
    row = ids_row[...]
    diagonal = down_i == over_i
    row_f = row.astype(f32)
    col_f = jnp.sum(jnp.where(diagonal, row_f, 0.0), axis=1, keepdims=True)
    weight_col = jnp.sum(jnp.where(diagonal, weight_row[...], 0.0), axis=1, keepdims=True)
    position = jnp.sum(
        jnp.where((col_f == row_f) & (down_i < over_i), 1.0, 0.0), axis=0, keepdims=True
    )
    target = row * cap + position.astype(jnp.int32)
    places = lax.broadcasted_iota(jnp.int32, (n_exp * cap, count), 0)
    table[...] = jnp.where(places == target, 1.0, 0.0).astype(bf)

    def exchange(source, out, sends, recvs, local, which):
        moves = [
            pltpu.make_async_remote_copy(
                src_ref=source.at[rows_of(peer)],
                dst_ref=out.at[rows_of(me_exp)],
                send_sem=sends.at[d, which],
                recv_sem=recvs.at[d, which],
                device_id={"exp": peer},
                device_id_type=MESH,
            )
            for d, peer in enumerate(exp_peers)
        ]
        moves.append(
            pltpu.make_async_copy(
                source.at[rows_of(me_exp)], out.at[rows_of(me_exp)], local.at[which]
            )
        )
        for one in moves:
            one.start()
        return moves

    send_x[...] = dot(table[...], tok[...], (((1,), (0,)), ((), ()))).astype(bf)
    sent_x = exchange(send_x, x_rows, d_send, d_recv, d_local, 0)
    scaled = (weight_col * cot[...].astype(f32)).astype(bf)
    send_y[...] = dot(table[...], scaled, (((1,), (0,)), ((), ()))).astype(bf)
    sent_y = exchange(send_y, y_rows, d_send, d_recv, d_local, 1)
    for g, one in zip(weights, own_weights):
        g.start(4)
        one.start()
    for g in weights:
        g.relay()
    for g in weights:
        g.share_near()

    def spread(source, out, which):
        moves = [
            pltpu.make_async_remote_copy(
                src_ref=source.at[:, columns(peer)],
                dst_ref=out.at[me],
                send_sem=m_send.at[d, which],
                recv_sem=m_recv.at[d, which],
                device_id={"ctx": peer},
                device_id_type=MESH,
            )
            for d, peer in enumerate(ctx_peers)
        ]
        moves.append(
            pltpu.make_async_copy(source.at[:, columns(me)], out.at[me], m_local.at[which])
        )
        for one in moves:
            one.start()
        return moves

    for one in sent_x:
        one.wait()
    moved = spread(x_rows, x_all, 0)

    def forward_x(c, start=False):
        xc = x_rows[:, columns(c)]
        for acc, weight in ((gate_acc, gate_w), (up_acc, up_w)):
            part = dot(xc, weight[c], (((1,), (0,)), ((), ())))
            acc[...] = part if start else acc[...] + part

    def forward_y(c, start=False):
        part = dot(y_rows[:, columns(c)], down_w[c], NT)
        back_acc[...] = part if start else back_acc[...] + part

    near = (sib, across, along, ctx_neighbours(across)[0], ctx_neighbours(along)[0])
    for one in own_weights:
        one.wait()
    forward_x(me, True)
    for g in weights:
        g.arrived(4)
        g.arrived(7, 8)
    weights[0].share_far()
    for c in near[:3]:
        forward_x(c)
    weights[1].share_far()
    for c in near[3:]:
        forward_x(c)
    weights[2].share_far()
    for one in sent_y:
        one.wait()
    moved = moved + spread(y_rows, y_all, 1)
    forward_y(me, True)
    for c in near:
        forward_y(c)
    forward_x(far)
    forward_y(far)
    for g in weights:
        g.arrived(9, 10)
    last = ctx_neighbours(far)[0]
    forward_x(last)
    forward_y(last)

    gate, up, back_sum = gate_acc[...], up_acc[...], back_acc[...]
    sig = 1.0 / (1.0 + jnp.exp(-gate))
    hidden = (gate * sig * up).astype(bf)
    hid_all[me] = hidden
    dg_all[me] = (back_sum * up * sig * (1.0 + gate * (1.0 - sig))).astype(bf)
    du_all[me] = (back_sum * gate * sig).astype(bf)
    states = [
        Gather(out.at[me], out, s_send.at[i], s_recv.at[i])
        for i, out in enumerate((hid_all, dg_all, du_all))
    ]
    for g in states:
        g.start(0, 1)
    for g in states:
        g.start(2, 3)
    for g in states:
        g.start(4)
    inner[...] = jnp.broadcast_to(
        jnp.sum(hidden.astype(f32) * back_sum, axis=1, keepdims=True), inner.shape
    )
    sent_inner = exchange(inner, home_inner, r_send, r_recv, r_local, 0)
    for c in range(n_ctx):
        back[:, c * cols:(c + 1) * cols] = (
            dot(dg_all[me], gate_w[c], NT) + dot(du_all[me], up_w[c], NT)
        ).astype(bf)
    sent_back = exchange(back, home, r_send, r_recv, r_local, 1)
    for g in states:
        g.relay()
    for g in states:
        g.share_near()
    for one in moved:
        one.wait()

    def fold(c, start):
        xc, yc = x_all[c], y_all[c]
        parts = (dot(yc, hid_all[c], TN), dot(xc, dg_all[c], TN), dot(xc, du_all[c], TN))
        for acc, part in zip((dn_acc, gg_acc, ug_acc), parts):
            acc[...] = part if start else acc[...] + part

    for g in states:
        g.arrived(4)
    fold(me, True)
    fold(sib, False)
    states[0].share_far()
    fold(across, False)
    states[1].share_far()
    fold(along, False)
    for g in states:
        g.arrived(7, 8)
    fold(ctx_neighbours(across)[0], False)
    fold(ctx_neighbours(along)[0], False)
    states[2].share_far()
    for one in sent_inner + sent_back:
        one.wait()
    token_out[...] = dot(table[...], home[...], TN).astype(bf)
    route_out[...] = (
        jnp.sum(table[...].astype(f32) * home_inner[...], axis=0, keepdims=True) / weight_row[...]
    )
    fold(far, False)
    for g in states:
        g.arrived(9, 10)
    fold(ctx_neighbours(far)[0], False)
    gate_grad[...] = gg_acc[...].astype(bf)
    up_grad[...] = ug_acc[...].astype(bf)
    down_grad[...] = dn_acc[...].T.astype(bf)
    for g in weights + states:
        g.sent()


def hand_over(*refs):
    for source, out in zip(refs[:5], refs[5:]):
        out[...] = source[...]


def fast_body(tokens, cotangent, expert_ids, route_weights, w_gate, w_up, w_down):
    n_ctx = lax.axis_size("ctx")
    n_exp = lax.axis_size("exp")
    count, width = tokens.shape
    cap = max(2, (3 * count + 2 * n_exp - 1) // (2 * n_exp))
    cols = width // n_ctx
    units = w_gate.shape[2]
    rows = n_exp * cap
    bf, f32 = jnp.bfloat16, jnp.float32
    vm = pl.BlockSpec(memory_space=pltpu.VMEM)
    hbm = pl.BlockSpec(memory_space=pl.ANY)
    dma = pltpu.SemaphoreType.DMA
    token_grads, route, gate_grads, up_grads, down_grads = pl.pallas_call(
        functools.partial(kernel, n_exp, n_ctx, cap),
        out_shape=(
            jax.ShapeDtypeStruct((count, width), bf),
            jax.ShapeDtypeStruct((1, count), f32),
            jax.ShapeDtypeStruct((cols, units), bf),
            jax.ShapeDtypeStruct((cols, units), bf),
            jax.ShapeDtypeStruct((units, cols), bf),
        ),
        in_specs=[vm] * 4 + [hbm] * 3,
        out_specs=(vm,) * 5,
        scratch_shapes=[pltpu.VMEM((rows, width), bf)] * 4
        + [
            pltpu.VMEM((n_ctx, cols, units), bf),
            pltpu.VMEM((n_ctx, cols, units), bf),
            pltpu.VMEM((n_ctx, units, cols), bf),
            pltpu.VMEM((rows, count), bf),
        ]
        + [pltpu.VMEM((rows, units), f32)] * 3
        + [pltpu.VMEM((n_ctx, rows, units), bf)] * 3
        + [pltpu.VMEM((n_ctx, rows, cols), bf)] * 2
        + [
            pltpu.VMEM((rows, width), bf),
            pltpu.VMEM((rows, count), f32),
            pltpu.VMEM((rows, width), bf),
            pltpu.VMEM((rows, count), f32),
        ]
        + [pltpu.VMEM((cols, units), f32)] * 3
        + [
            dma((3, 11)), dma((3, 11)), dma((3,)),
            dma((n_exp - 1, 2)), dma((n_exp - 1, 2)), dma((2,)),
            dma((3, 11)), dma((3, 11)),
            dma((n_ctx - 1, 2)), dma((n_ctx - 1, 2)), dma((2,)),
            dma((n_exp - 1, 2)), dma((n_exp - 1, 2)), dma((2,)),
        ],
        compiler_params=pltpu.CompilerParams(
            collective_id=0, has_side_effects=True, vmem_limit_bytes=56 * 1024 * 1024
        ),
    )(
        tokens, cotangent, expert_ids.reshape(1, count), route_weights.reshape(1, count),
        w_gate, w_up, w_down,
    )
    results = (token_grads, route, gate_grads, up_grads, down_grads)
    token_grads, route, gate_grads, up_grads, down_grads = pl.pallas_call(
        hand_over,
        out_shape=tuple(jax.ShapeDtypeStruct(r.shape, r.dtype) for r in results),
        in_specs=[vm] * 5,
        out_specs=(vm,) * 5,
    )(*results)
    return (
        token_grads, route.reshape(count, 1), gate_grads[None], up_grads[None], down_grads[None]
    )


def solution(mesh):
    return jax.shard_map(
        fast_body if mesh.shape["ctx"] == 8 else body,
        mesh=mesh,
        in_specs=(
            P(("ctx", "exp"), None),
            P(("ctx", "exp"), None),
            P(("ctx", "exp"), None),
            P(("ctx", "exp"), None),
            P("exp", "ctx", None),
            P("exp", "ctx", None),
            P("exp", None, "ctx"),
        ),
        out_specs=(
            P(("ctx", "exp"), None),
            P(("ctx", "exp"), None),
            P("exp", "ctx", None),
            P("exp", "ctx", None),
            P("exp", None, "ctx"),
        ),
        check_vma=False,
    )
```

```python
import functools

import jax
import jax.numpy as jnp
from jax import lax
from jax.experimental import pallas as pl
from jax.experimental.pallas import tpu as pltpu
from jax.sharding import PartitionSpec as P

MESH = pl.DeviceIdType.MESH


def slot_table(route_ids, expert_count, capacity):
    labels = jnp.arange(expert_count, dtype=jnp.int32)
    onehot = (route_ids[..., :, None] == labels).astype(jnp.int32)
    position = jnp.sum((jnp.cumsum(onehot, axis=-2) - 1) * onehot, axis=-1)
    target = route_ids * capacity + position
    places = jnp.arange(expert_count * capacity, dtype=jnp.int32)
    return (target[..., None, :] == places[:, None]).astype(jnp.bfloat16)


def forward_hidden(totals, units):
    gate_pre = totals[:, :units]
    up_pre = totals[:, units:]
    gate_sig = jax.nn.sigmoid(gate_pre)
    return (gate_pre * gate_sig * up_pre).astype(jnp.bfloat16)


def backward_grads(totals, back_sum, units):
    gate_pre = totals[:, :units]
    up_pre = totals[:, units:]
    gate_sig = jax.nn.sigmoid(gate_pre)
    d_up = (back_sum * gate_pre * gate_sig).astype(jnp.bfloat16)
    d_gate = (back_sum * up_pre * gate_sig * (1.0 + gate_pre * (1.0 - gate_sig))).astype(
        jnp.bfloat16
    )
    return jnp.concatenate([d_gate, d_up], axis=1)


def body(tokens, cotangent, expert_ids, route_weights, w_gate, w_up, w_down):
    ctx_size = lax.axis_size("ctx")
    exp_size = lax.axis_size("exp")
    tok_count, model_width = tokens.shape
    route_count = expert_ids.shape[1]
    slot_count = tok_count * route_count
    expert_count = w_gate.shape[0] * exp_size
    capacity = max(2, (3 * slot_count + 2 * expert_count - 1) // (2 * expert_count))
    col_count = model_width // ctx_size
    units = w_gate.shape[2]
    row_count = ctx_size * exp_size * capacity
    own_rows = row_count // ctx_size
    all_ids = lax.all_gather(expert_ids, "ctx", axis=0, tiled=True)
    tables = slot_table(all_ids.reshape(ctx_size, slot_count), expert_count, capacity)
    token_slots = jnp.repeat(tokens, route_count, axis=0)
    scaled = (
        route_weights * jnp.repeat(cotangent, route_count, axis=0).astype(jnp.float32)
    ).astype(jnp.bfloat16)
    own_table = lax.dynamic_index_in_dim(tables, lax.axis_index("ctx"), 0, keepdims=False)
    send_x = jnp.dot(own_table, token_slots, preferred_element_type=jnp.float32).astype(
        jnp.bfloat16
    )
    send_y = jnp.dot(own_table, scaled, preferred_element_type=jnp.float32).astype(jnp.bfloat16)
    send_x = send_x.reshape(expert_count, capacity, model_width)
    send_y = send_y.reshape(expert_count, capacity, model_width)
    group_x, group_y = (
        lax.all_to_all(send_x, "exp", split_axis=0, concat_axis=0, tiled=True),
        lax.all_to_all(send_y, "exp", split_axis=0, concat_axis=0, tiled=True),
    )
    slot_x, slot_y = (
        lax.all_to_all(group_x, "ctx", split_axis=2, concat_axis=0, tiled=True),
        lax.all_to_all(group_y, "ctx", split_axis=2, concat_axis=0, tiled=True),
    )
    slot_x = slot_x.reshape(row_count, col_count)
    slot_y = slot_y.reshape(row_count, col_count)
    gate_weight = w_gate[0]
    up_weight = w_up[0]
    down_weight = w_down[0]
    both_weights = jnp.concatenate([gate_weight, up_weight], axis=1)

    def fold_grad(segment):
        gate_acc = lax.dot_general(
            slot_x, segment[:, :units], (((0,), (0,)), ((), ())), preferred_element_type=jnp.float32
        )
        up_acc = lax.dot_general(
            slot_x, segment[:, units:], (((0,), (0,)), ((), ())), preferred_element_type=jnp.float32
        )
        grad_rows = lax.dot_general(
            segment, both_weights, (((1,), (1,)), ((), ())), preferred_element_type=jnp.float32
        )
        return (gate_acc, up_acc, grad_rows)

    row_x, row_y = (
        lax.all_to_all(slot_x, "ctx", split_axis=0, concat_axis=1, tiled=True),
        lax.all_to_all(slot_y, "ctx", split_axis=0, concat_axis=1, tiled=True),
    )
    full_gate, full_up, full_down = (
        lax.all_gather(gate_weight, "ctx", axis=0, tiled=True),
        lax.all_gather(up_weight, "ctx", axis=0, tiled=True),
        lax.all_gather(down_weight, "ctx", axis=1, tiled=True),
    )
    full_both = jnp.concatenate([full_gate, full_up], axis=1).reshape(
        ctx_size, col_count, 2 * units
    )
    gate_blocks = jnp.einsum(
        "rcd,cdf->crf",
        row_x.reshape(own_rows, ctx_size, col_count),
        full_both,
        preferred_element_type=jnp.float32,
    ).astype(jnp.bfloat16)
    totals_own = jnp.sum(gate_blocks.astype(jnp.float32), axis=0)
    hidden_own = forward_hidden(totals_own, units)
    back_blocks = jnp.einsum(
        "rcd,fcd->crf",
        row_y.reshape(own_rows, ctx_size, col_count),
        full_down.reshape(units, ctx_size, col_count),
        preferred_element_type=jnp.float32,
    ).astype(jnp.bfloat16)
    back_own = jnp.sum(back_blocks.astype(jnp.float32), axis=0)
    grads_own = backward_grads(totals_own, back_own, units)
    segment = (
        lax.all_gather(hidden_own, "ctx", axis=0, tiled=True),
        lax.all_gather(grads_own, "ctx", axis=0, tiled=True),
    )
    fold_segment = segment[0]
    outputs = jnp.dot(fold_segment, down_weight, preferred_element_type=jnp.float32)
    inner_rows = jnp.sum(slot_y.astype(jnp.float32) * outputs, axis=1)
    inner_all = inner_rows
    down_acc = lax.dot_general(
        fold_segment, slot_y, (((0,), (0,)), ((), ())), preferred_element_type=jnp.float32
    )
    down_state = (down_acc, inner_all)
    grad_state = fold_grad(segment[1])
    down_acc = down_state[0]
    inner_all = down_state[1]
    gate_acc = grad_state[0]
    up_acc = grad_state[1]
    back_rows = grad_state[2]
    back_slots = back_rows.astype(jnp.bfloat16).reshape(ctx_size, exp_size, capacity, col_count)
    inner_slots = inner_all.reshape(ctx_size, exp_size, capacity)
    home_back = lax.all_to_all(back_slots, "exp", split_axis=1, concat_axis=1, tiled=True)
    home_inner = lax.all_to_all(inner_slots, "exp", split_axis=1, concat_axis=1, tiled=True)
    merged = jnp.einsum(
        "cks,ckd->csd",
        tables,
        home_back.reshape(ctx_size, expert_count * capacity, col_count),
        preferred_element_type=jnp.float32,
    )
    merged = jnp.sum(merged.reshape(ctx_size, tok_count, route_count, col_count), axis=2).astype(
        jnp.bfloat16
    )
    grads_home = lax.all_to_all(merged, "ctx", split_axis=0, concat_axis=2, tiled=True)
    token_grads = grads_home.reshape(tok_count, model_width)
    inner_home = jnp.einsum(
        "cks,ck->cs",
        tables.astype(jnp.float32),
        home_inner.reshape(ctx_size, expert_count * capacity),
        precision=lax.Precision.HIGHEST,
    )
    route_sums = lax.psum_scatter(inner_home, "ctx", scatter_dimension=0, tiled=True).reshape(
        tok_count, route_count
    )
    route_grads = route_sums / route_weights
    gate_grads = gate_acc.astype(jnp.bfloat16)[None]
    up_grads = up_acc.astype(jnp.bfloat16)[None]
    down_grads = down_acc.astype(jnp.bfloat16)[None]
    return (token_grads, route_grads, gate_grads, up_grads, down_grads)


def ctx_neighbours(me):
    sib = me + 1 - 2 * (me % 2)
    across = me + 2 - 4 * ((me // 2) % 2)
    along = me + 4 - 8 * ((me // 4) % 2)
    return sib, across, along


def enter(ctx_peers, exp_peers):
    barrier = pltpu.get_barrier_semaphore()
    for peer in ctx_peers:
        pl.semaphore_signal(barrier, inc=1, device_id={"ctx": peer}, device_id_type=MESH)
    for peer in exp_peers:
        pl.semaphore_signal(barrier, inc=1, device_id={"exp": peer}, device_id_type=MESH)
    pl.semaphore_wait(barrier, len(ctx_peers) + len(exp_peers))


class Gather:
    def __init__(self, own, out, send_sem, recv_sem):
        me = lax.axis_index("ctx")
        sib, across, along = ctx_neighbours(me)
        half = own.shape[0] // 2
        first, second = pl.ds(0, half), pl.ds(half, half)
        far = ctx_neighbours(across)[2]

        def copy(k, source, target, peer):
            return pltpu.make_async_remote_copy(
                src_ref=source,
                dst_ref=target,
                send_sem=send_sem.at[k],
                recv_sem=recv_sem.at[k],
                device_id={"ctx": peer},
                device_id_type=MESH,
            )

        self.c = [
            copy(0, own.at[first], out.at[me, first], across),
            copy(1, own.at[second], out.at[me, second], along),
            copy(2, own.at[second], out.at[me, second], across),
            copy(3, own.at[first], out.at[me, first], along),
            copy(4, own, out.at[me], sib),
            copy(5, out.at[across, first], out.at[across, first], along),
            copy(6, out.at[along, second], out.at[along, second], across),
            copy(7, out.at[across], out.at[across], sib),
            copy(8, out.at[along], out.at[along], sib),
            copy(9, out.at[far, first], out.at[far, first], sib),
            copy(10, out.at[far, second], out.at[far, second], sib),
        ]

    def start(self, *which):
        for k in which:
            self.c[k].start()

    def arrived(self, *which):
        for k in which:
            self.c[k].wait_recv()

    def relay(self):
        self.arrived(0)
        self.start(5)
        self.arrived(1)
        self.start(6)

    def share_near(self):
        self.arrived(2)
        self.start(7)
        self.arrived(3)
        self.start(8)

    def share_far(self):
        self.arrived(5)
        self.start(9)
        self.arrived(6)
        self.start(10)

    def sent(self):
        for one in self.c:
            one.wait_send()


NT = (((1,), (1,)), ((), ()))
TN = (((0,), (0,)), ((), ()))


def dot(a, b, dims):
    return lax.dot_general(a, b, dims, preferred_element_type=jnp.float32)


def kernel(
    n_exp, n_ctx, cap,
    tok_in, cot_in, ids_row, weight_row, w_gate, w_up, w_down,
    token_out, route_out, gate_grad, up_grad, down_grad,
    send_x, send_y, x_rows, y_rows, gate_w, up_w, down_w, table,
    gate_acc, up_acc, back_acc, hid_all, dg_all, du_all, x_all, y_all,
    back, inner, home, home_inner, gg_acc, ug_acc, dn_acc,
    w_send, w_recv, w_local, d_send, d_recv, d_local,
    s_send, s_recv, m_send, m_recv, m_local, r_send, r_recv, r_local,
    tok, cot, in_sem,
):
    me_exp = lax.axis_index("exp")
    me = lax.axis_index("ctx")
    bf, f32 = jnp.bfloat16, jnp.float32
    sib, across, along = ctx_neighbours(me)
    far = ctx_neighbours(across)[2]
    exp_peers = [lax.rem(me_exp + d, n_exp) for d in range(1, n_exp)]
    ctx_peers = [lax.rem(me + d, n_ctx) for d in range(1, n_ctx)]
    loads = [
        pltpu.make_async_copy(tok_in, tok, in_sem.at[0]),
        pltpu.make_async_copy(cot_in, cot, in_sem.at[1]),
    ]
    for one in loads:
        one.start()
    enter(ctx_peers, exp_peers)

    weights = [
        Gather(own.at[0], out, w_send.at[i], w_recv.at[i])
        for i, (own, out) in enumerate(((w_gate, gate_w), (w_up, up_w), (w_down, down_w)))
    ]
    own_weights = [
        pltpu.make_async_copy(own.at[0], out.at[me], w_local.at[i])
        for i, (own, out) in enumerate(((w_gate, gate_w), (w_up, up_w), (w_down, down_w)))
    ]
    for g in weights:
        g.start(0, 1)
    for g in weights:
        g.start(2, 3)

    count, width = tok.shape
    cols = width // n_ctx

    def rows_of(at):
        return pl.ds(pl.multiple_of(at * cap, cap), cap)

    def columns(at):
        return pl.ds(pl.multiple_of(at * cols, cols), cols)

    down_i = lax.broadcasted_iota(jnp.int32, (count, count), 0)
    over_i = lax.broadcasted_iota(jnp.int32, (count, count), 1)
    row = ids_row[...]
    diagonal = down_i == over_i
    row_f = row.astype(f32)
    col_f = jnp.sum(jnp.where(diagonal, row_f, 0.0), axis=1, keepdims=True)
    weight_col = jnp.sum(jnp.where(diagonal, weight_row[...], 0.0), axis=1, keepdims=True)
    position = jnp.sum(
        jnp.where((col_f == row_f) & (down_i < over_i), 1.0, 0.0), axis=0, keepdims=True
    )
    target = row * cap + position.astype(jnp.int32)
    places = lax.broadcasted_iota(jnp.int32, (n_exp * cap, count), 0)
    table[...] = jnp.where(places == target, 1.0, 0.0).astype(bf)

    def exchange(source, out, sends, recvs, local, which):
        moves = [
            pltpu.make_async_remote_copy(
                src_ref=source.at[rows_of(peer)],
                dst_ref=out.at[rows_of(me_exp)],
                send_sem=sends.at[d, which],
                recv_sem=recvs.at[d, which],
                device_id={"exp": peer},
                device_id_type=MESH,
            )
            for d, peer in enumerate(exp_peers)
        ]
        moves.append(
            pltpu.make_async_copy(
                source.at[rows_of(me_exp)], out.at[rows_of(me_exp)], local.at[which]
            )
        )
        for one in moves:
            one.start()
        return moves

    loads[0].wait()
    send_x[...] = dot(table[...], tok[...], (((1,), (0,)), ((), ()))).astype(bf)
    sent_x = exchange(send_x, x_rows, d_send, d_recv, d_local, 0)
    loads[1].wait()
    scaled = (weight_col * cot[...].astype(f32)).astype(bf)
    send_y[...] = dot(table[...], scaled, (((1,), (0,)), ((), ()))).astype(bf)
    sent_y = exchange(send_y, y_rows, d_send, d_recv, d_local, 1)
    for g, one in zip(weights, own_weights):
        g.start(4)
        one.start()
    for g in weights:
        g.relay()
    for g in weights:
        g.share_near()

    def spread(source, out, which):
        moves = [
            pltpu.make_async_remote_copy(
                src_ref=source.at[:, columns(peer)],
                dst_ref=out.at[me],
                send_sem=m_send.at[d, which],
                recv_sem=m_recv.at[d, which],
                device_id={"ctx": peer},
                device_id_type=MESH,
            )
            for d, peer in enumerate(ctx_peers)
        ]
        moves.append(
            pltpu.make_async_copy(source.at[:, columns(me)], out.at[me], m_local.at[which])
        )
        for one in moves:
            one.start()
        return moves

    for one in sent_x:
        one.wait()
    moved = spread(x_rows, x_all, 0)

    def forward_x(c, start=False):
        xc = x_rows[:, columns(c)]
        for acc, weight in ((gate_acc, gate_w), (up_acc, up_w)):
            part = dot(xc, weight[c], (((1,), (0,)), ((), ())))
            acc[...] = part if start else acc[...] + part

    def forward_y(c, start=False):
        part = dot(y_rows[:, columns(c)], down_w[c], NT)
        back_acc[...] = part if start else back_acc[...] + part

    near = (sib, across, along, ctx_neighbours(across)[0], ctx_neighbours(along)[0])
    for one in own_weights:
        one.wait()
    forward_x(me, True)
    for g in weights:
        g.arrived(4)
        g.arrived(7, 8)
    weights[0].share_far()
    for c in near[:3]:
        forward_x(c)
    weights[1].share_far()
    for c in near[3:]:
        forward_x(c)
    weights[2].share_far()
    for one in sent_y:
        one.wait()
    moved = moved + spread(y_rows, y_all, 1)
    forward_y(me, True)
    for c in near:
        forward_y(c)
    forward_x(far)
    forward_y(far)
    for g in weights:
        g.arrived(9, 10)
    last = ctx_neighbours(far)[0]
    forward_x(last)
    forward_y(last)

    gate, up, back_sum = gate_acc[...], up_acc[...], back_acc[...]
    sig = 1.0 / (1.0 + jnp.exp(-gate))
    hidden = (gate * sig * up).astype(bf)
    states = [
        Gather(out.at[me], out, s_send.at[i], s_recv.at[i])
        for i, out in enumerate((hid_all, dg_all, du_all))
    ]
    hid_all[me] = hidden
    states[0].start(0, 1)
    dg_all[me] = (back_sum * up * sig * (1.0 + gate * (1.0 - sig))).astype(bf)
    states[1].start(0, 1)
    du_all[me] = (back_sum * gate * sig).astype(bf)
    states[2].start(0, 1)
    for g in states:
        g.start(2, 3)
    for g in states:
        g.start(4)
    inner[...] = jnp.broadcast_to(
        jnp.sum(hidden.astype(f32) * back_sum, axis=1, keepdims=True), inner.shape
    )
    sent_inner = exchange(inner, home_inner, r_send, r_recv, r_local, 0)
    for c in range(n_ctx):
        back[:, c * cols:(c + 1) * cols] = (
            dot(dg_all[me], gate_w[c], NT) + dot(du_all[me], up_w[c], NT)
        ).astype(bf)
    sent_back = exchange(back, home, r_send, r_recv, r_local, 1)
    for g in states:
        g.relay()
    for g in states:
        g.share_near()
    for one in moved:
        one.wait()

    def fold(c, start):
        xc, yc = x_all[c], y_all[c]
        parts = (dot(yc, hid_all[c], TN), dot(xc, dg_all[c], TN), dot(xc, du_all[c], TN))
        for acc, part in zip((dn_acc, gg_acc, ug_acc), parts):
            acc[...] = part if start else acc[...] + part

    for g in states:
        g.arrived(4)
    fold(me, True)
    fold(sib, False)
    states[0].share_far()
    fold(across, False)
    states[1].share_far()
    fold(along, False)
    for g in states:
        g.arrived(7, 8)
    fold(ctx_neighbours(across)[0], False)
    fold(ctx_neighbours(along)[0], False)
    states[2].share_far()
    for one in sent_inner + sent_back:
        one.wait()
    token_out[...] = dot(table[...], home[...], TN).astype(bf)
    route_out[...] = (
        jnp.sum(table[...].astype(f32) * home_inner[...], axis=0, keepdims=True) / weight_row[...]
    )
    fold(far, False)
    for g in states:
        g.arrived(9, 10)
    fold(ctx_neighbours(far)[0], False)
    gate_grad[...] = gg_acc[...].astype(bf)
    up_grad[...] = ug_acc[...].astype(bf)
    down_grad[...] = dn_acc[...].T.astype(bf)
    for g in weights + states:
        g.sent()


def hand_over(*refs):
    for source, out in zip(refs[:5], refs[5:]):
        out[...] = source[...]


def fast_body(tokens, cotangent, expert_ids, route_weights, w_gate, w_up, w_down):
    n_ctx = lax.axis_size("ctx")
    n_exp = lax.axis_size("exp")
    count, width = tokens.shape
    cap = max(2, (3 * count + 2 * n_exp - 1) // (2 * n_exp))
    cols = width // n_ctx
    units = w_gate.shape[2]
    rows = n_exp * cap
    bf, f32 = jnp.bfloat16, jnp.float32
    vm = pl.BlockSpec(memory_space=pltpu.VMEM)
    hbm = pl.BlockSpec(memory_space=pl.ANY)
    dma = pltpu.SemaphoreType.DMA
    token_grads, route, gate_grads, up_grads, down_grads = pl.pallas_call(
        functools.partial(kernel, n_exp, n_ctx, cap),
        out_shape=(
            jax.ShapeDtypeStruct((count, width), bf),
            jax.ShapeDtypeStruct((1, count), f32),
            jax.ShapeDtypeStruct((cols, units), bf),
            jax.ShapeDtypeStruct((cols, units), bf),
            jax.ShapeDtypeStruct((units, cols), bf),
        ),
        in_specs=[hbm] * 2 + [vm] * 2 + [hbm] * 3,
        out_specs=(vm,) * 5,
        scratch_shapes=[pltpu.VMEM((rows, width), bf)] * 4
        + [
            pltpu.VMEM((n_ctx, cols, units), bf),
            pltpu.VMEM((n_ctx, cols, units), bf),
            pltpu.VMEM((n_ctx, units, cols), bf),
            pltpu.VMEM((rows, count), bf),
        ]
        + [pltpu.VMEM((rows, units), f32)] * 3
        + [pltpu.VMEM((n_ctx, rows, units), bf)] * 3
        + [pltpu.VMEM((n_ctx, rows, cols), bf)] * 2
        + [
            pltpu.VMEM((rows, width), bf),
            pltpu.VMEM((rows, count), f32),
            pltpu.VMEM((rows, width), bf),
            pltpu.VMEM((rows, count), f32),
        ]
        + [pltpu.VMEM((cols, units), f32)] * 3
        + [
            dma((3, 11)), dma((3, 11)), dma((3,)),
            dma((n_exp - 1, 2)), dma((n_exp - 1, 2)), dma((2,)),
            dma((3, 11)), dma((3, 11)),
            dma((n_ctx - 1, 2)), dma((n_ctx - 1, 2)), dma((2,)),
            dma((n_exp - 1, 2)), dma((n_exp - 1, 2)), dma((2,)),
            pltpu.VMEM((count, width), bf), pltpu.VMEM((count, width), bf), dma((2,)),
        ],
        compiler_params=pltpu.CompilerParams(
            collective_id=0, has_side_effects=True, vmem_limit_bytes=56 * 1024 * 1024
        ),
    )(
        tokens, cotangent, expert_ids.reshape(1, count), route_weights.reshape(1, count),
        w_gate, w_up, w_down,
    )
    results = (token_grads, route, gate_grads, up_grads, down_grads)
    token_grads, route, gate_grads, up_grads, down_grads = pl.pallas_call(
        hand_over,
        out_shape=tuple(jax.ShapeDtypeStruct(r.shape, r.dtype) for r in results),
        in_specs=[vm] * 5,
        out_specs=(vm,) * 5,
    )(*results)
    return (
        token_grads, route.reshape(count, 1), gate_grads[None], up_grads[None], down_grads[None]
    )


def solution(mesh):
    return jax.shard_map(
        fast_body if mesh.shape["ctx"] == 8 else body,
        mesh=mesh,
        in_specs=(
            P(("ctx", "exp"), None),
            P(("ctx", "exp"), None),
            P(("ctx", "exp"), None),
            P(("ctx", "exp"), None),
            P("exp", "ctx", None),
            P("exp", "ctx", None),
            P("exp", None, "ctx"),
        ),
        out_specs=(
            P(("ctx", "exp"), None),
            P(("ctx", "exp"), None),
            P("exp", "ctx", None),
            P("exp", "ctx", None),
            P("exp", None, "ctx"),
        ),
        check_vma=False,
    )
```
